256 devices in a mesh: dp: 4 (over y), entity: 64 (over z, x, core).
Axes of the slice: x: 4, y: 4, z: 8, core: 2. Of those that a mesh axis runs over, the one named last changes fastest.
Arguments:
- entities: float32 [64, 4096, 256], P('entity'), may hold values from -20 to 20
- relations: float32 [256, 256, 256], P('entity'), may hold values from -0.375 to 0.375
- candidate_blocks: int32 [256, 8], P('dp'), may hold values from 0 to 63, as said below
- list_lengths: int32 [4, 64], P('dp'), may hold values from 2 to 8, as said below
- head_offsets: int32 [32768], P(('dp', 'entity')), may hold values from 0 to 4095
- relation_offsets: int32 [32768], P(('dp', 'entity')), may hold values from 0 to 3
- target_codes: int32 [32768], P(('dp', 'entity')), may hold values from 0 to 32767
Outputs:
- loss: float32 [32768], P(('dp', 'entity'))
- entity_grad: float32 [64, 4096, 256], P('entity', 'dp')
The draws below stay inside these ranges and needn't reach their ends.
Inputs may be any that keep to these rules, and one draw needn't show every extreme that they name: `candidate_blocks`: each row names 8 different blocks. Among the entries of the 64 rows of one dp group, used or not, no block is named more than 12 times; in every dp group one block is named exactly 12 times, each time at a used entry. `list_lengths`: the 64 lengths of one dp group sum to 320, and one of them is 8.
All inputs are finite; a program needn't handle non-finite values.
Results may differ from the reference program's by a relative error of at most 0.0025.
The reference program's roundings to bfloat16 on the way count: a program that leaves them out, or rounds other values in their place, can miss the bound.
Values may be sent and summed in bfloat16 or wider, within the bound.
No kernel may reach another device: no remote copies, remote signals or barrier semaphores. Data moves between devices by JAX's collectives and lax.ppermute only.
A program may use at most 64 MiB of HBM per device.

```python
import jax
import jax.numpy as jnp
from jax import lax

D = 256
RELS = 256
BLOCK = 4096
TOP = 8
TRIP_DEV = 128
NBLOCKS = 64
REL_DEV = 4
SETS = 256
TRIPLES = 32768
MOST = 12
N_DP = 4
N_ENTITY = 64


def draw_entities(key, part):
    first, second = jax.random.split(key, 2)
    base = jnp.clip(jax.random.normal(first, (NBLOCKS, BLOCK, D), jnp.float32), -6.0, 6.0)
    scales = jnp.exp(jax.random.uniform(second, (NBLOCKS, BLOCK, 1), jnp.float32, -0.4, 0.4))
    values = 0.35 * base * scales
    return values


def draw_lists(key):
    group_total = SETS // NBLOCKS
    row_total = NBLOCKS
    half_total = row_total // 2

    def one_group(group_key):
        order_key, shuffle_key, row_key, length_key, place_key = jax.random.split(group_key, 5)
        block_order = jax.random.permutation(order_key, row_total).astype(jnp.int32)
        row_index = jnp.arange(row_total, dtype=jnp.int32)
        column = jnp.arange(TOP, dtype=jnp.int32)
        position = (row_index[:, None] + column[None, :]) % row_total
        holds = position == 0
        contains = jnp.any(holds, axis=1)
        extra = (row_index >= 1) & (row_index <= MOST - TOP)
        crowded = contains | extra
        leading = position[:, :1]
        swapped = jnp.where(holds, leading, position)
        lead_column = (column[None, :] == 0) & crowded[:, None]
        placed = jnp.where(lead_column, 0, swapped)
        scores = jax.random.randint(shuffle_key, (row_total, TOP), 0, 1024, dtype=jnp.int32) * TOP + column[None, :]
        scores = jnp.where(lead_column, -1, scores)
        ordering = jnp.argsort(scores, axis=1, stable=True)
        shuffled = jnp.take_along_axis(placed, ordering, axis=1)
        named = jnp.take(block_order, shuffled)
        row_order = jax.random.permutation(row_key, row_total)
        named = jnp.take(named, row_order, axis=0)
        firsts = jax.random.randint(length_key, (half_total,), 2, TOP + 1, dtype=jnp.int32)
        firsts = jnp.where(jnp.arange(half_total, dtype=jnp.int32) == 0, TOP, firsts)
        paired = jnp.stack([firsts, 10 - firsts], axis=1).reshape(row_total)
        length_order = jax.random.permutation(place_key, row_total)
        return (named.astype(jnp.int32), jnp.take(paired, length_order).astype(jnp.int32))
    named, lengths = jax.vmap(one_group)(jax.random.split(key, group_total))
    return (named.reshape(group_total * row_total, TOP), lengths)


def draw_candidate_blocks(key, part):
    return draw_lists(jax.random.fold_in(key, 7))[0]


def draw_list_lengths(key, part):
    return draw_lists(jax.random.fold_in(key, 7))[1]


def set_ends(entries, rng, smallest, top_value):
    extent = entries.shape
    index_at = [jax.random.randint(jax.random.fold_in(rng, axis), (), 0, extent[axis]) for axis in range(len(extent))]
    entries = entries.at[tuple(index_at)].set(smallest)
    longest = extent.index(max(extent))
    index_at[longest] = (index_at[longest] + 1) % extent[longest]
    return entries.at[tuple(index_at)].set(top_value)


def level_of(rng, shape, shards, least, largest):
    loudness, own = 1.0, jax.random.fold_in(rng, 6)
    for axis_at, parts in shards:
        steps = jnp.exp(jax.random.uniform(jax.random.fold_in(own, axis_at), (parts,), jnp.float32, least / len(shards), largest / len(shards)))
        loudness = loudness * jnp.repeat(steps, shape[axis_at] // parts).reshape([-1 if axis == axis_at else 1 for axis in range(len(shape))])
    return loudness


def centred(key, extent, spread, bound, shards=(), held_as=jnp.bfloat16):
    result = jax.random.normal(key, extent, jnp.float32) * spread
    if len(shards) > 0:
        result = level_of(key, extent, shards, -0.22, 0.18) * result
    return jnp.clip(result, min=-bound, max=bound).astype(held_as)


def setup_inputs(seed: int = 0) -> dict:
    key_of = jax.random.split(jax.random.key(seed), 8)
    return {
        "entities": draw_entities(jax.random.fold_in(key_of[7], 71), 0),
        "relations": centred(key_of[1], (RELS, D, D), D ** -0.5, 0.375, ((0, 64),), jnp.float32),
        "candidate_blocks": draw_candidate_blocks(jax.random.fold_in(key_of[7], 71), 0),
        "list_lengths": draw_list_lengths(jax.random.fold_in(key_of[7], 71), 0),
        "head_offsets": set_ends(jax.random.randint(key_of[4], (TRIPLES,), 0, BLOCK), jax.random.fold_in(key_of[4], 1), 0, BLOCK - 1).astype(jnp.int32),
        "relation_offsets": set_ends(jax.random.randint(key_of[5], (TRIPLES,), 0, REL_DEV), jax.random.fold_in(key_of[5], 1), 0, REL_DEV - 1).astype(jnp.int32),
        "target_codes": set_ends(jax.random.randint(key_of[6], (TRIPLES,), 0, TOP * BLOCK), jax.random.fold_in(key_of[6], 1), 0, (TOP * BLOCK) - 1).astype(jnp.int32),
    }


negative_floor = -1e30


def combine_stats(earlier, latter):
    first_max, first_sum, first_target = earlier
    second_max, second_sum, second_target = latter
    larger = jnp.maximum(first_max, second_max)
    combined = first_sum * jnp.exp(first_max - larger) + second_sum * jnp.exp(second_max - larger)
    return (larger, combined, first_target + second_target)


def keep_value(current):
    return current


def reference(entities, relations, candidate_blocks, list_lengths, head_offsets, relation_offsets, target_codes):
    set_total = N_DP * N_ENTITY
    local_relations = RELS // N_ENTITY
    lengths = list_lengths.reshape(set_total)
    head_grid = head_offsets.reshape(set_total, TRIP_DEV)
    kind_grid = relation_offsets.reshape(set_total, TRIP_DEV)
    code_grid = target_codes.reshape(set_total, TRIP_DEV)
    rounded = lax.optimization_barrier(entities.astype(jnp.bfloat16))

    def make_query(set_number):
        home = set_number % N_ENTITY
        table = lax.dynamic_index_in_dim(entities, home, 0, keepdims=False)
        head_rows = jnp.take(table, head_grid[set_number], axis=0)
        chosen = lax.dynamic_slice_in_dim(relations, home * local_relations, local_relations, 0)
        products = jnp.einsum("td,rde->tre", head_rows, chosen, precision=lax.Precision.HIGHEST)
        selector = (kind_grid[set_number][:, None] == jnp.arange(local_relations, dtype=jnp.int32)[None, :]).astype(jnp.float32)
        return jnp.sum(products * selector[:, :, None], axis=1).astype(jnp.bfloat16)

    queries = lax.map(make_query, jnp.arange(set_total, dtype=jnp.int32))
    picks = ((code_grid // BLOCK) % lengths[:, None]).astype(jnp.int32)
    target_block = jnp.take_along_axis(candidate_blocks, picks, axis=1)
    target_row = (code_grid % BLOCK).astype(jnp.int32)
    positions = jnp.arange(BLOCK, dtype=jnp.int32)

    def block_scores(query_full, block):
        keys = lax.dynamic_index_in_dim(rounded, block, 0, keepdims=False).astype(jnp.float32)
        return jnp.dot(query_full, keys.T, precision=lax.Precision.HIGHEST)

    def target_mask(set_number, block):
        same_block = target_block[set_number][:, None] == block
        return same_block & (positions[None, :] == target_row[set_number][:, None])

    def set_stats(set_number):
        query_full = queries[set_number].astype(jnp.float32)

        def visit(carry, entry):
            def include(current):
                block = candidate_blocks[set_number, entry]
                scores = block_scores(query_full, block)
                maxima = jnp.max(scores, axis=1)
                masses = jnp.sum(jnp.exp(scores - maxima[:, None]), axis=1)
                picked = jnp.sum(jnp.where(target_mask(set_number, block), scores, 0.0), axis=1)
                return combine_stats(current, (maxima, masses, picked))
            return lax.cond(entry < lengths[set_number], include, keep_value, carry), None

        initial = (jnp.full((TRIP_DEV,), negative_floor, jnp.float32), jnp.zeros((TRIP_DEV,), jnp.float32), jnp.zeros((TRIP_DEV,), jnp.float32))
        final, unused = lax.scan(visit, initial, jnp.arange(TOP, dtype=jnp.int32))
        return final

    maxima, masses, picked = lax.map(set_stats, jnp.arange(set_total, dtype=jnp.int32))
    log_norm = maxima + jnp.log(masses)
    loss = (log_norm - picked).reshape(-1)

    def set_grads(gradient, set_number):
        query_full = queries[set_number].astype(jnp.float32)
        norm_row = log_norm[set_number]

        def visit(current, entry):
            block = candidate_blocks[set_number, entry]

            def include(unused_value):
                scores = block_scores(query_full, block)
                weights = jnp.exp(scores - norm_row[:, None])
                coefficients = (weights - target_mask(set_number, block).astype(jnp.float32)).astype(jnp.bfloat16)
                coefficients = lax.optimization_barrier(coefficients).astype(jnp.float32)
                return jnp.dot(coefficients.T, query_full, precision=lax.Precision.HIGHEST)

            def nothing(unused_value):
                return jnp.zeros((BLOCK, D), jnp.float32)

            update = lax.cond(entry < lengths[set_number], include, nothing, 0)
            previous = lax.dynamic_index_in_dim(current, block, 0, keepdims=False)
            return lax.dynamic_update_index_in_dim(current, previous + update, block, 0), None

        gradient, unused = lax.scan(visit, gradient, jnp.arange(TOP, dtype=jnp.int32))
        return gradient, None

    gradient, unused = lax.scan(set_grads, jnp.zeros((NBLOCKS, BLOCK, D), jnp.float32), jnp.arange(set_total, dtype=jnp.int32))
    return (loss, gradient)
```

```python
import jax
import jax.numpy as jnp
from jax import lax
from jax.experimental import pallas as pl
from jax.experimental.pallas import tpu as pltpu
from jax.sharding import PartitionSpec as P

f32, bf16, i32 = jnp.float32, jnp.bfloat16, jnp.int32
CAP = 12
HALF = CAP // 2
NEG = -1e30
HIGH = lax.Precision.HIGHEST
VMEM_BYTES = 56 * 1024 * 1024


def iota(shape, axis):
    return lax.broadcasted_iota(i32, shape, axis)


def dot(a, b, ca=1, cb=0, precision=None):
    return lax.dot_general(
        a, b, (((ca,), (cb,)), ((), ())), precision=precision, preferred_element_type=f32
    )


def whole(shape):
    return pl.BlockSpec(shape, lambda *_: (0,) * len(shape))


def query_kernel(heads, table, relations, kinds, codes, lists, lengths, out, ranks, rows, sem):
    count = rows.shape[0]
    sets = lists.shape[0]

    def fetch(n, carry):
        pltpu.make_async_copy(
            table.at[pl.ds(heads[n], 1), :], rows.at[pl.ds(n, 1), :], sem
        ).start()
        return carry

    lax.fori_loop(0, count, fetch, 0, unroll=8)
    listed_t = dot(
        lists[...].astype(f32).astype(bf16),
        (iota((sets, sets), 0) == iota((sets, sets), 1)).astype(f32).astype(bf16),
        0,
        0,
    )
    entry = iota(listed_t.shape, 0)
    listed_t = jnp.where(entry < lengths[...], listed_t, -1.0)
    block = iota((sets, sets), 0).astype(f32)
    listed = jnp.zeros((sets, sets), f32)
    for k in range(listed_t.shape[0]):
        listed = jnp.where(listed_t[k : k + 1, :] == block, 1.0, listed)
    before = (iota((sets, sets), 0) < iota((sets, sets), 1)).astype(f32).astype(bf16)
    rank = dot(listed.astype(bf16), before)
    ranks[...] = jnp.where(listed > 0.0, rank, -1.0)
    diagonal = iota((count, count), 0) == iota((count, count), 1)
    kind = jnp.sum(jnp.where(diagonal, kinds[...].astype(f32), 0.0), axis=1, keepdims=True)
    pltpu.make_async_copy(table.at[pl.ds(0, count), :], rows, sem).wait()
    head = rows[...]
    query = jnp.zeros((count, relations.shape[2]), f32)
    for r in range(relations.shape[0]):
        product = dot(head, relations[r], precision=HIGH)
        query = jnp.where(kind == r, product, query)
    query = query.astype(bf16)
    total, width = out.shape[0], query.shape[1]
    row, column = iota((total, width), 0), iota((total, width), 1)
    pick = (row % 8 < 4) & (row // 8 * 4 + row % 8 == column)
    spread = dot(pick.astype(f32).astype(bf16), query, 1, 1)
    row = iota(spread.shape, 0) % 8
    code = codes[...]
    spread = jnp.where(row == 4, (code // 128).astype(f32), spread)
    spread = jnp.where(row == 5, (code % 128).astype(f32), spread)
    out[...] = spread.astype(bf16)


def pack_kernel(me, ranks, held, lists, lengths, out, targets, sets_rows):
    sets = ranks.shape[0]
    size = held.shape[0]
    rank = ranks[...]
    up = (iota((size, sets), 0) // 8 == iota((size, sets), 1)).astype(f32).astype(bf16)
    wide = dot(up, rank.astype(bf16))
    wide = dot(wide.astype(bf16), up, 1, 1)
    row, column = iota((size, size), 0), iota((size, size), 1)
    wide = jnp.where(row % 4 == column % 8, wide - (row % 8 // 4 * HALF).astype(f32), NEG)
    listed = dot(dot(up, (rank >= 0.0).astype(f32).astype(bf16)).astype(bf16), up, 1, 1) > 0.5
    wide = jnp.where(listed, wide, NEG)
    values = held[...]
    lanes = values.shape[1]
    for i in range(HALF):
        chosen = (wide == float(i)).astype(f32).astype(bf16)
        out[:, i * lanes : (i + 1) * lanes] = dot(chosen, values).astype(bf16)
    mine = ranks[pl.ds(me[0], 1), :]
    slots = targets.shape[0]
    slot = iota((slots, sets), 0).astype(f32)
    taken = mine == slot
    onehot = taken.astype(f32).astype(bf16)
    expanded = dot(onehot, up, 1, 1)
    column = iota(expanded.shape, 1) % 8
    high = dot(jnp.where(column == 4, expanded, 0.0).astype(bf16), values).astype(i32)
    low = dot(jnp.where(column == 5, expanded, 0.0).astype(bf16), values).astype(i32)
    code = high * 128 + low
    used = jnp.sum(taken.astype(f32), axis=1, keepdims=True) > 0.5
    length = jnp.sum(jnp.where(taken, lengths[...].astype(f32), 0.0), axis=1, keepdims=True).astype(i32)
    slot_lists = dot(onehot, lists[...].astype(f32).astype(bf16)).astype(i32)
    entry = code // sets_rows
    for _ in range(3):
        entry = jnp.where(entry >= length, entry - length, entry)
    block = jnp.full(code.shape, -1, i32)
    for k in range(slot_lists.shape[1]):
        block = jnp.where(entry == k, slot_lists[:, k : k + 1], block)
    here = (block == me[0]) & used
    targets[...] = jnp.where(here, code % sets_rows, -1)


def stats_kernel(
    me, ranks, received, table, targets, query_t, query, out, top_s, sum_s, tgt_s
):
    step = pl.program_id(0)
    pairs = CAP // 2
    width = 256
    tile = table.shape[0]

    @pl.when(step == 0)
    def _():
        size = received.shape[0]
        half = size // 2
        lanes = received.shape[1]
        values = received[...]
        row, column = iota((half, size), 0), iota((half, size), 1)
        for h in range(2):
            pick = (row // 4 * 8 + h * 4 + row % 4 == column).astype(f32).astype(bf16)
            query_t[:, h * lanes : (h + 1) * lanes] = dot(pick, values).astype(bf16)
            query[h * lanes : (h + 1) * lanes, :] = dot(values, pick, 0, 1).astype(bf16)
        top_s[...] = jnp.full(top_s.shape, NEG, f32)
        sum_s[...] = jnp.zeros(sum_s.shape, f32)
        tgt_s[...] = jnp.zeros(tgt_s.shape, f32)

    rows = table[...].astype(bf16)
    place = iota((tile, width), 0) + step * tile
    for p in range(pairs):
        columns = slice(p * width, (p + 1) * width)
        score = dot(rows, query_t[:, columns])
        target = jnp.concatenate([targets[2 * p : 2 * p + 1, :], targets[2 * p + 1 : 2 * p + 2, :]], axis=1)
        grouped = score.reshape(tile // 8, 8, width)
        old = top_s[:, columns]
        top = jnp.maximum(old, jnp.max(grouped, axis=0))
        mass = jnp.sum(jnp.exp(grouped - top[None]), axis=0)
        sum_s[:, columns] = sum_s[:, columns] * jnp.exp(old - top) + mass
        top_s[:, columns] = top
        hit = jnp.where(place == target, score, 0.0).reshape(tile // 8, 8, width)
        tgt_s[:, columns] = tgt_s[:, columns] + jnp.sum(hit, axis=0)

    @pl.when(step == pl.num_programs(0) - 1)
    def _():
        top = top_s[...]
        best = jnp.max(top, axis=0, keepdims=True)
        mass = jnp.sum(sum_s[...] * jnp.exp(top - best), axis=0, keepdims=True)
        local = best + jnp.log(mass)
        picked = jnp.sum(tgt_s[...], axis=0, keepdims=True)
        blank = jnp.zeros((4, 128), f32)
        stacked = jnp.concatenate(
            [local[:, i * 128 : (i + 1) * 128] for i in range(CAP)]
            + [blank]
            + [picked[:, i * 128 : (i + 1) * 128] for i in range(CAP)]
            + [blank],
            axis=0,
        )
        sets = ranks.shape[0]
        total = out.shape[0]
        rank = ranks[...]
        up = (iota((total, sets), 0) // 16 == iota((total, sets), 1)).astype(f32)
        wide = dot(up.astype(bf16), rank.astype(bf16))
        slot = iota((total, sets), 0) % 16
        shared = (wide == slot.astype(f32)) & (slot < CAP)
        shared = shared | (((slot == CAP) | (slot == CAP + 1)) & (up > 0.5))
        mine = ranks[pl.ds(me[0], 1), :]
        owned = mine == (iota((32, sets), 0) % 16).astype(f32)
        match = dot(shared.astype(f32).astype(bf16), owned.astype(f32).astype(bf16), 1, 1)
        slot, source = iota((total, 32), 0) % 16, iota((total, 32), 1)
        match = jnp.where((slot == CAP + 1) == (source >= 16), match, 0.0)
        picked_rows = dot(match, stacked, precision=HIGH)
        present = dot(match.astype(bf16), jnp.ones((32, 128), bf16))
        missing = jnp.where(iota((total, 128), 0) % 16 == CAP + 1, 0.0, NEG)
        out[...] = jnp.where(present > 0.5, picked_rows, missing)


def merge_kernel(received, norms, loss):
    values = received[...]
    best = jnp.max(values, axis=0)
    mass = jnp.sum(jnp.exp(values - best[None]), axis=0)
    norm = best + jnp.log(mass)
    norms[...] = jnp.where(best <= 0.5 * NEG, -NEG, norm)
    target = jnp.sum(values[:, CAP + 1, :], axis=0, keepdims=True)
    loss[...] = norm[CAP : CAP + 1, :] - target


def grads_kernel(first, norms, targets, table, query_t, query, out, coefficients):
    step = pl.program_id(0)
    tile = table.shape[0]
    width = 256
    rows = table[...].astype(bf16)
    place = iota((tile, width), 0) + (first[0] * (pl.num_programs(0) * tile) + step * tile)
    for p in range(CAP // 2):
        columns = slice(p * width, (p + 1) * width)
        score = dot(rows, query_t[:, columns])
        norm = jnp.concatenate([norms[2 * p : 2 * p + 1, :], norms[2 * p + 1 : 2 * p + 2, :]], axis=1)
        target = jnp.concatenate([targets[2 * p : 2 * p + 1, :], targets[2 * p + 1 : 2 * p + 2, :]], axis=1)
        weight = jnp.exp(score - norm)
        coefficients[:, columns] = jnp.where(place == target, weight - 1.0, weight).astype(bf16)
    out[...] = dot(coefficients[...], query[...]).astype(out.dtype)


def per_device(
    entities,
    relations,
    candidate_blocks,
    list_lengths,
    head_offsets,
    relation_offsets,
    target_codes,
):
    owners = lax.axis_size("entity")
    groups = lax.axis_size("dp")
    table = entities[0]
    block_rows, depth = table.shape
    count = head_offsets.shape[0]
    me = lax.axis_index("entity").astype(i32).reshape(1)
    group = lax.axis_index("dp").astype(i32)
    smem = pl.BlockSpec(memory_space=pltpu.SMEM)
    params = pltpu.CompilerParams(vmem_limit_bytes=VMEM_BYTES)
    kinds = relation_offsets.reshape(1, count)
    codes = target_codes.reshape(1, count)

    spread, ranks = pl.pallas_call(
        query_kernel,
        out_shape=(
            jax.ShapeDtypeStruct((owners * 8, count), bf16),
            jax.ShapeDtypeStruct((owners, owners), f32),
        ),
        in_specs=[smem, pl.BlockSpec(memory_space=pl.ANY)] + [pl.BlockSpec(memory_space=pltpu.VMEM)] * 5,
        scratch_shapes=[pltpu.VMEM((count, depth), f32), pltpu.SemaphoreType.DMA],
        compiler_params=params,
        name="query",
    )(head_offsets, table, relations, kinds, codes, candidate_blocks, list_lengths)

    held = lax.all_to_all(spread.reshape(owners, 8, count), "entity", 0, 0, tiled=True)

    def pack(*refs):
        pack_kernel(*refs, block_rows)

    packed, targets = pl.pallas_call(
        pack,
        out_shape=(
            jax.ShapeDtypeStruct((owners * 8, HALF * count), bf16),
            jax.ShapeDtypeStruct((16, count), i32),
        ),
        in_specs=[smem] + [pl.BlockSpec(memory_space=pltpu.VMEM)] * 4,
        compiler_params=params,
        name="pack",
    )(me, ranks, held.reshape(owners * 8, count), candidate_blocks, list_lengths)

    received = lax.all_to_all(packed.reshape(owners, 8, HALF * count), "entity", 0, 0, tiled=True)

    tile = 1024
    query_t, query, local = pl.pallas_call(
        stats_kernel,
        grid=(block_rows // tile,),
        out_shape=(
            jax.ShapeDtypeStruct((depth, CAP * count), bf16),
            jax.ShapeDtypeStruct((CAP * count, depth), bf16),
            jax.ShapeDtypeStruct((owners * 16, count), f32),
        ),
        in_specs=[
            smem,
            whole((owners, owners)),
            whole((owners * 8, HALF * count)),
            pl.BlockSpec((tile, depth), lambda s: (s, 0)),
            whole((16, count)),
        ],
        out_specs=[whole((depth, CAP * count)), whole((CAP * count, depth)), whole((owners * 16, count))],
        scratch_shapes=[pltpu.VMEM((8, CAP * count), f32)] * 3,
        compiler_params=params,
        name="stats",
    )(me, ranks, received.reshape(owners * 8, HALF * count), table, targets)

    shared = lax.all_to_all(local.reshape(owners, 16, count), "entity", 0, 0, tiled=True)

    norms, loss = pl.pallas_call(
        merge_kernel,
        out_shape=(jax.ShapeDtypeStruct((16, count), f32), jax.ShapeDtypeStruct((1, count), f32)),
        compiler_params=params,
        name="merge",
    )(shared)

    quarter = block_rows // groups
    tile = 512

    def grads(which, dtype):
        return pl.pallas_call(
            grads_kernel,
            grid_spec=pltpu.PrefetchScalarGridSpec(
                num_scalar_prefetch=1,
                grid=(quarter // tile,),
                in_specs=[
                    pl.BlockSpec((16, count), lambda s, w: (0, 0)),
                    pl.BlockSpec((16, count), lambda s, w: (0, 0)),
                    pl.BlockSpec((tile, depth), lambda s, w: (w[0] * (quarter // tile) + s, 0)),
                    pl.BlockSpec((depth, CAP * count), lambda s, w: (0, 0)),
                    pl.BlockSpec((CAP * count, depth), lambda s, w: (0, 0)),
                ],
                out_specs=pl.BlockSpec((tile, depth), lambda s, w: (s, 0)),
                scratch_shapes=[pltpu.VMEM((tile, CAP * count), bf16)],
            ),
            out_shape=jax.ShapeDtypeStruct((quarter, depth), dtype),
            compiler_params=params,
            name="grads",
        )(which.reshape(1), norms, targets, table, query_t, query)

    arrived = []
    for shift in (2, 1, 3):
        part = grads((group + shift) % groups, bf16)
        arrived.append(lax.ppermute(part, "dp", [(i, (i + shift) % groups) for i in range(groups)]))
    gradient = grads(group, f32)
    for part in arrived:
        gradient = gradient + part.astype(f32)
    return (loss.reshape(count), gradient[None])


def solution(mesh):
    return jax.shard_map(
        per_device,
        mesh=mesh,
        in_specs=(
            P("entity", None, None),
            P("entity", None, None),
            P("dp", None),
            P("dp", None),
            P(("dp", "entity")),
            P(("dp", "entity")),
            P(("dp", "entity")),
        ),
        out_specs=(P(("dp", "entity")), P("entity", "dp", None)),
        check_vma=False,
    )
```

```python
import jax
import jax.numpy as jnp
from jax import lax
from jax.experimental import pallas as pl
from jax.experimental.pallas import tpu as pltpu
from jax.sharding import PartitionSpec as P

f32, bf16, i32 = jnp.float32, jnp.bfloat16, jnp.int32
CAP = 12
HALF = CAP // 2
NEG = -1e30
HIGH = lax.Precision.HIGHEST


def iota(shape, axis):
    return lax.broadcasted_iota(i32, shape, axis)


def dot(a, b, ca=1, cb=0, precision=None):
    return lax.dot_general(
        a, b, (((ca,), (cb,)), ((), ())), precision=precision, preferred_element_type=f32
    )


def whole(shape):
    return pl.BlockSpec(shape, lambda *_: (0,) * len(shape))


def query_kernel(heads, table, relations, kinds, codes, lists, lengths, out, ranks, rows, sem):
    count = rows.shape[0]
    sets = lists.shape[1]

    def fetch(n, carry):
        pltpu.make_async_copy(
            table.at[pl.ds(heads[n], 1), :], rows.at[pl.ds(n, 1), :], sem
        ).start()
        return carry

    lax.fori_loop(0, count, fetch, 0, unroll=8)
    listed_t = lists[...].astype(f32)
    listed_t = jnp.where(iota(listed_t.shape, 0) < lengths[...], listed_t, -1.0)
    block = iota((sets, sets), 0).astype(f32)
    listed = jnp.zeros((sets, sets), f32)
    for k in range(listed_t.shape[0]):
        listed = jnp.where(listed_t[k : k + 1, :] == block, 1.0, listed)
    before = (iota((sets, sets), 0) < iota((sets, sets), 1)).astype(f32).astype(bf16)
    rank = dot(listed.astype(bf16), before)
    ranks[...] = jnp.where(listed > 0.0, rank, -1.0)
    diagonal = iota((count, count), 0) == iota((count, count), 1)
    kind = jnp.sum(jnp.where(diagonal, kinds[...].astype(f32), 0.0), axis=1, keepdims=True)
    pltpu.make_async_copy(table.at[pl.ds(0, count), :], rows, sem).wait()
    head = rows[...]
    query = jnp.zeros((count, relations.shape[2]), f32)
    for r in range(relations.shape[0]):
        product = dot(head, relations[r], precision=HIGH)
        query = jnp.where(kind == r, product, query)
    query = query.astype(bf16)
    total, width = out.shape[0], query.shape[1]
    row, column = iota((total, width), 0), iota((total, width), 1)
    pick = (row % 8 < 4) & (row // 8 * 4 + row % 8 == column)
    spread = dot(pick.astype(f32).astype(bf16), query, 1, 1)
    row = iota(spread.shape, 0) % 8
    code = codes[...]
    spread = jnp.where(row == 4, (code // 128).astype(f32), spread)
    spread = jnp.where(row == 5, (code % 128).astype(f32), spread)
    out[...] = spread.astype(bf16)


def pack_kernel(me, ranks, held, lists, lengths, out, targets, sets_rows):
    sets = ranks.shape[0]
    size = held.shape[0]
    rank = ranks[...]
    up = (iota((size, sets), 0) // 8 == iota((size, sets), 1)).astype(f32).astype(bf16)
    wide = dot(up, rank.astype(bf16))
    wide = dot(wide.astype(bf16), up, 1, 1)
    row, column = iota((size, size), 0), iota((size, size), 1)
    wide = jnp.where(row % 4 == column % 8, wide - (row % 8 // 4 * HALF).astype(f32), NEG)
    listed = dot(dot(up, (rank >= 0.0).astype(f32).astype(bf16)).astype(bf16), up, 1, 1) > 0.5
    wide = jnp.where(listed, wide, NEG)
    values = held[...]
    lanes = values.shape[1]
    for i in range(HALF):
        chosen = (wide == float(i)).astype(f32).astype(bf16)
        out[:, i * lanes : (i + 1) * lanes] = dot(chosen, values).astype(bf16)
    mine = ranks[pl.ds(me[0], 1), :]
    slots = targets.shape[0]
    slot = iota((slots, sets), 0).astype(f32)
    taken = mine == slot
    onehot = taken.astype(f32).astype(bf16)
    expanded = dot(onehot, up, 1, 1)
    column = iota(expanded.shape, 1) % 8
    high = dot(jnp.where(column == 4, expanded, 0.0).astype(bf16), values).astype(i32)
    low = dot(jnp.where(column == 5, expanded, 0.0).astype(bf16), values).astype(i32)
    code = high * 128 + low
    used = jnp.sum(taken.astype(f32), axis=1, keepdims=True) > 0.5
    length = jnp.sum(jnp.where(taken, lengths[...].astype(f32), 0.0), axis=1, keepdims=True).astype(i32)
    slot_lists = dot(onehot, lists[...].astype(f32).astype(bf16), 1, 1).astype(i32)
    entry = code // sets_rows
    for _ in range(3):
        entry = jnp.where(entry >= length, entry - length, entry)
    block = jnp.full(code.shape, -1, i32)
    for k in range(slot_lists.shape[1]):
        block = jnp.where(entry == k, slot_lists[:, k : k + 1], block)
    here = (block == me[0]) & used
    targets[...] = jnp.where(here, code % sets_rows, -1)


def stats_kernel(
    me, ranks, received, table, targets, query_t, query, out, top_s, sum_s, tgt_s
):
    step = pl.program_id(0)
    pairs = CAP // 2
    width = 256
    tile = table.shape[0]

    @pl.when(step == 0)
    def _():
        size = received.shape[0]
        half = size // 2
        lanes = received.shape[1]
        values = received[...]
        row, column = iota((half, size), 0), iota((half, size), 1)
        for h in range(2):
            pick = (row // 4 * 8 + h * 4 + row % 4 == column).astype(f32).astype(bf16)
            query_t[:, h * lanes : (h + 1) * lanes] = dot(pick, values).astype(bf16)
            query[h * lanes : (h + 1) * lanes, :] = dot(values, pick, 0, 1).astype(bf16)
        top_s[...] = jnp.full(top_s.shape, NEG, f32)
        sum_s[...] = jnp.zeros(sum_s.shape, f32)
        tgt_s[...] = jnp.zeros(tgt_s.shape, f32)

    rows = table[...].astype(bf16)
    place = iota((tile, width), 0) + step * tile
    for p in range(pairs):
        columns = slice(p * width, (p + 1) * width)
        score = dot(rows, query_t[:, columns])
        target = jnp.concatenate([targets[2 * p : 2 * p + 1, :], targets[2 * p + 1 : 2 * p + 2, :]], axis=1)
        grouped = score.reshape(tile // 8, 8, width)
        old = top_s[:, columns]
        top = jnp.maximum(old, jnp.max(grouped, axis=0))
        mass = jnp.sum(jnp.exp(grouped - top[None]), axis=0)
        sum_s[:, columns] = sum_s[:, columns] * jnp.exp(old - top) + mass
        top_s[:, columns] = top
        hit = jnp.where(place == target, score, 0.0).reshape(tile // 8, 8, width)
        tgt_s[:, columns] = tgt_s[:, columns] + jnp.sum(hit, axis=0)

    @pl.when(step == pl.num_programs(0) - 1)
    def _():
        top = top_s[...]
        best = jnp.max(top, axis=0, keepdims=True)
        mass = jnp.sum(sum_s[...] * jnp.exp(top - best), axis=0, keepdims=True)
        local = best + jnp.log(mass)
        picked = jnp.sum(tgt_s[...], axis=0, keepdims=True)
        blank = jnp.zeros((4, 128), f32)
        stacked = jnp.concatenate(
            [local[:, i * 128 : (i + 1) * 128] for i in range(CAP)]
            + [blank]
            + [picked[:, i * 128 : (i + 1) * 128] for i in range(CAP)]
            + [blank],
            axis=0,
        )
        sets = ranks.shape[0]
        total = out.shape[0]
        rank = ranks[...]
        up = (iota((total, sets), 0) // 16 == iota((total, sets), 1)).astype(f32)
        wide = dot(up.astype(bf16), rank.astype(bf16))
        slot = iota((total, sets), 0) % 16
        shared = (wide == slot.astype(f32)) & (slot < CAP)
        shared = shared | (((slot == CAP) | (slot == CAP + 1)) & (up > 0.5))
        mine = ranks[pl.ds(me[0], 1), :]
        owned = mine == (iota((32, sets), 0) % 16).astype(f32)
        match = dot(shared.astype(f32).astype(bf16), owned.astype(f32).astype(bf16), 1, 1)
        slot, source = iota((total, 32), 0) % 16, iota((total, 32), 1)
        match = jnp.where((slot == CAP + 1) == (source >= 16), match, 0.0)
        picked_rows = dot(match, stacked, precision=HIGH)
        present = dot(match.astype(bf16), jnp.ones((32, 128), bf16))
        missing = jnp.where(iota((total, 128), 0) % 16 == CAP + 1, 0.0, NEG)
        out[...] = jnp.where(present > 0.5, picked_rows, missing)


def merge_kernel(received, norms, loss):
    values = received[...]
    best = jnp.max(values, axis=0)
    mass = jnp.sum(jnp.exp(values - best[None]), axis=0)
    norm = best + jnp.log(mass)
    norms[...] = jnp.where(best <= 0.5 * NEG, -NEG, norm)
    target = jnp.sum(values[:, CAP + 1, :], axis=0, keepdims=True)
    loss[...] = norm[CAP : CAP + 1, :] - target


def grads_kernel(first, norms, targets, table, query_t, query, out, coefficients):
    step = pl.program_id(0)
    tile = table.shape[0]
    width = 256
    rows = table[...].astype(bf16)
    place = iota((tile, width), 0) + (first[0] * (pl.num_programs(0) * tile) + step * tile)
    for p in range(CAP // 2):
        columns = slice(p * width, (p + 1) * width)
        score = dot(rows, query_t[:, columns])
        norm = jnp.concatenate([norms[2 * p : 2 * p + 1, :], norms[2 * p + 1 : 2 * p + 2, :]], axis=1)
        target = jnp.concatenate([targets[2 * p : 2 * p + 1, :], targets[2 * p + 1 : 2 * p + 2, :]], axis=1)
        weight = jnp.exp(score - norm)
        coefficients[:, columns] = jnp.where(place == target, weight - 1.0, weight).astype(bf16)
    out[...] = dot(coefficients[...], query[...]).astype(out.dtype)


def per_device(
    entities,
    relations,
    candidate_blocks,
    list_lengths,
    head_offsets,
    relation_offsets,
    target_codes,
):
    owners = lax.axis_size("entity")
    groups = lax.axis_size("dp")
    table = entities[0]
    block_rows, depth = table.shape
    count = head_offsets.shape[0]
    me = lax.axis_index("entity").astype(i32).reshape(1)
    group = lax.axis_index("dp").astype(i32)
    smem = pl.BlockSpec(memory_space=pltpu.SMEM)

    def params(mebibytes):
        return pltpu.CompilerParams(vmem_limit_bytes=mebibytes * 1024 * 1024)

    lists = candidate_blocks.T
    kinds = relation_offsets.reshape(1, count)
    codes = target_codes.reshape(1, count)

    spread, ranks = pl.pallas_call(
        query_kernel,
        out_shape=(
            jax.ShapeDtypeStruct((owners * 8, count), bf16),
            jax.ShapeDtypeStruct((owners, owners), f32),
        ),
        in_specs=[smem, pl.BlockSpec(memory_space=pltpu.HBM)] + [pl.BlockSpec(memory_space=pltpu.VMEM)] * 5,
        scratch_shapes=[pltpu.VMEM((count, depth), f32), pltpu.SemaphoreType.DMA],
        compiler_params=params(60),
        name="query",
    )(head_offsets, table, relations, kinds, codes, lists, list_lengths)

    held = lax.all_to_all(spread.reshape(owners, 8, count), "entity", 0, 0, tiled=True)

    def pack(*refs):
        pack_kernel(*refs, block_rows)

    packed, targets = pl.pallas_call(
        pack,
        out_shape=(
            jax.ShapeDtypeStruct((owners * 8, HALF * count), bf16),
            jax.ShapeDtypeStruct((16, count), i32),
        ),
        in_specs=[smem] + [pl.BlockSpec(memory_space=pltpu.VMEM)] * 4,
        compiler_params=params(12),
        name="pack",
    )(me, ranks, held.reshape(owners * 8, count), lists, list_lengths)

    received = lax.all_to_all(packed.reshape(owners, 8, HALF * count), "entity", 0, 0, tiled=True)

    tile = 1024
    query_t, query, local = pl.pallas_call(
        stats_kernel,
        grid=(block_rows // tile,),
        out_shape=(
            jax.ShapeDtypeStruct((depth, CAP * count), bf16),
            jax.ShapeDtypeStruct((CAP * count, depth), bf16),
            jax.ShapeDtypeStruct((owners * 16, count), f32),
        ),
        in_specs=[
            smem,
            whole((owners, owners)),
            whole((owners * 8, HALF * count)),
            pl.BlockSpec((tile, depth), lambda s: (s, 0)),
            whole((16, count)),
        ],
        out_specs=[whole((depth, CAP * count)), whole((CAP * count, depth)), whole((owners * 16, count))],
        scratch_shapes=[pltpu.VMEM((8, CAP * count), f32)] * 3,
        compiler_params=params(60),
        name="stats",
    )(me, ranks, received.reshape(owners * 8, HALF * count), table, targets)

    shared = lax.all_to_all(local.reshape(owners, 16, count), "entity", 0, 0, tiled=True)

    norms, loss = pl.pallas_call(
        merge_kernel,
        out_shape=(jax.ShapeDtypeStruct((16, count), f32), jax.ShapeDtypeStruct((1, count), f32)),
        compiler_params=params(8),
        name="merge",
    )(shared)

    quarter = block_rows // groups
    tile = 512

    def grads(which, dtype, norms):
        return pl.pallas_call(
            grads_kernel,
            grid_spec=pltpu.PrefetchScalarGridSpec(
                num_scalar_prefetch=1,
                grid=(quarter // tile,),
                in_specs=[
                    pl.BlockSpec((16, count), lambda s, w: (0, 0)),
                    pl.BlockSpec((16, count), lambda s, w: (0, 0)),
                    pl.BlockSpec((tile, depth), lambda s, w: (w[0] * (quarter // tile) + s, 0)),
                    pl.BlockSpec((depth, CAP * count), lambda s, w: (0, 0)),
                    pl.BlockSpec((CAP * count, depth), lambda s, w: (0, 0)),
                ],
                out_specs=pl.BlockSpec((tile, depth), lambda s, w: (s, 0)),
                scratch_shapes=[pltpu.VMEM((tile, CAP * count), bf16)],
            ),
            out_shape=jax.ShapeDtypeStruct((quarter, depth), dtype),
            compiler_params=params(60),
            cost_estimate=pl.CostEstimate(
                flops=4 * quarter * CAP * count * depth,
                transcendentals=quarter * CAP * count,
                bytes_accessed=4 * quarter * depth * 2 + 4 * CAP * count * depth,
            ),
            name="grads",
        )(which.reshape(1), norms, targets, table, query_t, query)

    arrived = []
    for shift in (2, 1, 3):
        part = grads((group + shift) % groups, bf16, norms)
        arrived.append(lax.ppermute(part, "dp", [(i, (i + shift) % groups) for i in range(groups)]))
    last_norms, arrived[0] = lax.optimization_barrier((norms, arrived[0]))
    gradient = grads(group, f32, last_norms)
    for part in arrived:
        gradient = gradient + part.astype(f32)
    return (loss.reshape(count), gradient[None])


def solution(mesh):
    return jax.shard_map(
        per_device,
        mesh=mesh,
        in_specs=(
            P("entity", None, None),
            P("entity", None, None),
            P("dp", None),
            P("dp", None),
            P(("dp", "entity")),
            P(("dp", "entity")),
            P(("dp", "entity")),
        ),
        out_specs=(P(("dp", "entity")), P("entity", "dp", None)),
        check_vma=False,
    )
```

```python
import jax
import jax.numpy as jnp
from jax import lax
from jax.experimental import pallas as pl
from jax.experimental.pallas import tpu as pltpu
from jax.sharding import PartitionSpec as P

f32, bf16, i32 = jnp.float32, jnp.bfloat16, jnp.int32
CAP = 12
HALF = CAP // 2
WIDE = 4
TILE = 1024
CHUNK = 128
NEG = -1e30
HIGH = lax.Precision.HIGHEST


def iota(shape, axis):
    return lax.broadcasted_iota(i32, shape, axis)


def dot(a, b, ca=1, cb=0, precision=None):
    return lax.dot_general(
        a, b, (((ca,), (cb,)), ((), ())), precision=precision, preferred_element_type=f32
    )


def whole(shape):
    return pl.BlockSpec(shape, lambda *_: (0,) * len(shape))


def query_kernel(heads, table, relations, kinds, codes, lists, lengths, out, ranks, rows, sem):
    count = rows.shape[0]
    sets = lists.shape[1]

    def fetch(n, carry):
        pltpu.make_async_copy(
            table.at[pl.ds(heads[n], 1), :], rows.at[pl.ds(n, 1), :], sem
        ).start()
        return carry

    lax.fori_loop(0, count, fetch, 0, unroll=8)
    listed_t = lists[...].astype(f32)
    listed_t = jnp.where(iota(listed_t.shape, 0) < lengths[...], listed_t, -1.0)
    block = iota((sets, sets), 0).astype(f32)
    listed = jnp.zeros((sets, sets), f32)
    for k in range(listed_t.shape[0]):
        listed = jnp.where(listed_t[k : k + 1, :] == block, 1.0, listed)
    before = (iota((sets, sets), 0) < iota((sets, sets), 1)).astype(f32).astype(bf16)
    rank = dot(listed.astype(bf16), before)
    ranks[...] = jnp.where(listed > 0.0, rank, -1.0)
    diagonal = iota((count, count), 0) == iota((count, count), 1)
    kind = jnp.sum(jnp.where(diagonal, kinds[...].astype(f32), 0.0), axis=1, keepdims=True)
    pltpu.make_async_copy(table.at[pl.ds(0, count), :], rows, sem).wait()
    head = rows[...]
    query = jnp.zeros((count, relations.shape[2]), f32)
    for r in range(relations.shape[0]):
        product = dot(head, relations[r], precision=HIGH)
        query = jnp.where(kind == r, product, query)
    query = query.astype(bf16)
    total, width = out.shape[0], query.shape[1]
    row, column = iota((total, width), 0), iota((total, width), 1)
    pick = (row % 8 < 4) & (row // 8 * 4 + row % 8 == column)
    spread = dot(pick.astype(f32).astype(bf16), query, 1, 1)
    row = iota(spread.shape, 0) % 8
    code = codes[...]
    spread = jnp.where(row == 4, (code // 128).astype(f32), spread)
    spread = jnp.where(row == 5, (code % 128).astype(f32), spread)
    out[...] = spread.astype(bf16)


def pack_kernel(me, ranks, held, lists, lengths, out, targets, sets_rows):
    sets = ranks.shape[0]
    size = held.shape[0]
    rank = ranks[...]
    up = (iota((size, sets), 0) // 8 == iota((size, sets), 1)).astype(f32).astype(bf16)
    wide = dot(up, rank.astype(bf16))
    wide = dot(wide.astype(bf16), up, 1, 1)
    row, column = iota((size, size), 0), iota((size, size), 1)
    wide = jnp.where(row % 4 == column % 8, wide - (row % 8 // 4 * HALF).astype(f32), NEG)
    listed = dot(dot(up, (rank >= 0.0).astype(f32).astype(bf16)).astype(bf16), up, 1, 1) > 0.5
    wide = jnp.where(listed, wide, NEG)
    values = held[...]
    lanes = values.shape[1]
    for i in range(HALF):
        chosen = (wide == float(i)).astype(f32).astype(bf16)
        out[:, i * lanes : (i + 1) * lanes] = dot(chosen, values).astype(bf16)
    mine = ranks[pl.ds(me[0], 1), :]
    slots = targets.shape[0]
    slot = iota((slots, sets), 0).astype(f32)
    taken = mine == slot
    onehot = taken.astype(f32).astype(bf16)
    expanded = dot(onehot, up, 1, 1)
    column = iota(expanded.shape, 1) % 8
    high = dot(jnp.where(column == 4, expanded, 0.0).astype(bf16), values).astype(i32)
    low = dot(jnp.where(column == 5, expanded, 0.0).astype(bf16), values).astype(i32)
    code = high * 128 + low
    used = jnp.sum(taken.astype(f32), axis=1, keepdims=True) > 0.5
    length = jnp.sum(jnp.where(taken, lengths[...].astype(f32), 0.0), axis=1, keepdims=True).astype(i32)
    slot_lists = dot(onehot, lists[...].astype(f32).astype(bf16), 1, 1).astype(i32)
    entry = code // sets_rows
    for _ in range(3):
        entry = jnp.where(entry >= length, entry - length, entry)
    block = jnp.full(code.shape, -1, i32)
    for k in range(slot_lists.shape[1]):
        block = jnp.where(entry == k, slot_lists[:, k : k + 1], block)
    here = (block == me[0]) & used
    targets[...] = jnp.where(here, code % sets_rows, -1)


def stats_kernel(received, table, targets, query_t, out, top_s, sum_s, tgt_s):
    size, lanes = received.shape
    half = size // 2
    values = received[...]
    row, column = iota((half, size), 0), iota((half, size), 1)
    for h in range(2):
        pick = (row // 4 * 8 + h * 4 + row % 4 == column).astype(f32).astype(bf16)
        query_t[:, h * lanes : (h + 1) * lanes] = dot(pick, values).astype(bf16)
    top_s[...] = jnp.full(top_s.shape, NEG, f32)
    sum_s[...] = jnp.zeros(sum_s.shape, f32)
    tgt_s[...] = jnp.zeros(tgt_s.shape, f32)

    def visit(step, carry):
        rows = table[pl.ds(step * TILE, TILE), :]
        for p in range(CAP // WIDE):
            columns = slice(p * WIDE * 128, (p + 1) * WIDE * 128)
            weights = query_t[:, columns]
            target = slot_lanes(targets, p)
            wanted = target - iota((8, target.shape[1]), 0) - step * TILE
            top, mass, hit = top_s[:, columns], sum_s[:, columns], tgt_s[:, columns]
            for c in range(TILE // CHUNK):
                score = dot(rows[c * CHUNK : (c + 1) * CHUNK, :], weights)
                score = score.reshape(CHUNK // 8, 8, score.shape[1])
                above = jnp.maximum(top, jnp.max(score, axis=0))
                mass = mass * jnp.exp(top - above) + jnp.sum(jnp.exp(score - above[None]), axis=0)
                top = above
                for k in range(CHUNK // 8):
                    hit = jnp.where(wanted == c * CHUNK + k * 8, score[k], hit)
            top_s[:, columns], sum_s[:, columns], tgt_s[:, columns] = top, mass, hit
        return carry

    lax.fori_loop(0, table.shape[0] // TILE, visit, 0)
    top = top_s[...]
    best = jnp.max(top, axis=0, keepdims=True)
    mass = jnp.sum(sum_s[...] * jnp.exp(top - best), axis=0, keepdims=True)
    local = best + jnp.log(mass)
    picked = jnp.sum(tgt_s[...], axis=0, keepdims=True)
    out[...] = jnp.zeros(out.shape, f32)
    for i in range(CAP):
        out[i : i + 1, :] = local[:, i * 128 : (i + 1) * 128]
        out[16 + i : 17 + i, :] = picked[:, i * 128 : (i + 1) * 128]


def slot_lanes(ref, p):
    return jnp.concatenate([ref[i : i + 1, :] for i in range(WIDE * p, WIDE * p + WIDE)], axis=1)


def share_kernel(me, ranks, mine, other, out):
    sets = ranks.shape[0]
    total = out.shape[0]
    core = me[0] % 2
    rank = ranks[...]
    row = iota((total, sets), 0)
    place = row // 16 * 2 + core
    up = (place == iota((total, sets), 1)).astype(f32)
    wide = dot(up.astype(bf16), rank.astype(bf16))
    slot = row % 16
    shared = (wide == slot.astype(f32)) & (slot < CAP)
    shared = shared | (((slot == CAP) | (slot == CAP + 1)) & (up > 0.5))
    shared = shared.astype(f32).astype(bf16)
    slot, source = iota((total, 32), 0) % 16, iota((total, 32), 1)
    keep = (slot == CAP + 1) == (source >= 16)
    wants_target = iota((total, 128), 0) % 16 == CAP + 1

    def rows_of(owner, values):
        owned = ranks[pl.ds(owner, 1), :] == (iota((32, sets), 0) % 16).astype(f32)
        match = jnp.where(keep, dot(shared, owned.astype(f32).astype(bf16), 1, 1), 0.0)
        found = dot(match, values[...], precision=HIGH)
        present = dot(match.astype(bf16), jnp.ones((32, 128), bf16))
        return jnp.where(present > 0.5, found, jnp.where(wants_target, 0.0, NEG))

    first = rows_of(me[0], mine)
    second = rows_of(me[0] + 1 - 2 * core, other)
    best = jnp.maximum(first, second)
    both = best + jnp.log(jnp.exp(first - best) + jnp.exp(second - best))
    out[...] = jnp.where(wants_target, first + second, both)


def merge_kernel(received, norms, loss):
    values = received[...]
    best = jnp.max(values, axis=0)
    mass = jnp.sum(jnp.exp(values - best[None]), axis=0)
    norm = best + jnp.log(mass)
    norms[...] = jnp.where(best <= 0.5 * NEG, -NEG, norm)
    target = jnp.sum(values[:, CAP + 1, :], axis=0, keepdims=True)
    loss[...] = norm[CAP : CAP + 1, :] - target


def grads_kernel(first, norms, targets, table, query_t, out, coefficients):
    count = out.shape[0]
    start = pl.multiple_of(first[0] * count, count)
    rows = table[pl.ds(start, count), :]
    for p in range(CAP // WIDE):
        columns = slice(p * WIDE * 128, (p + 1) * WIDE * 128)
        weights = query_t[:, columns]
        norm = slot_lanes(norms, p)
        target = slot_lanes(targets, p)
        wanted = target - iota((8, target.shape[1]), 0) - start
        for c in range(count // CHUNK):
            score = dot(rows[c * CHUNK : (c + 1) * CHUNK, :], weights)
            score = score.reshape(CHUNK // 8, 8, score.shape[1])
            weight = jnp.exp(score - norm[None])
            place = iota(score.shape, 0) * 8 + c * CHUNK
            weight = jnp.where(place == wanted[None], weight - 1.0, weight)
            coefficients[c * CHUNK : (c + 1) * CHUNK, columns] = weight.reshape(CHUNK, -1).astype(bf16)
    out[...] = dot(coefficients[...], query_t[...], 1, 1).astype(out.dtype)


def per_device(
    entities,
    relations,
    candidate_blocks,
    list_lengths,
    head_offsets,
    relation_offsets,
    target_codes,
):
    owners = lax.axis_size("entity")
    groups = lax.axis_size("dp")
    table = entities[0]
    block_rows, depth = table.shape
    count = head_offsets.shape[0]
    me = lax.axis_index("entity").astype(i32).reshape(1)
    group = lax.axis_index("dp").astype(i32)
    smem = pl.BlockSpec(memory_space=pltpu.SMEM)

    def params(mebibytes):
        return pltpu.CompilerParams(vmem_limit_bytes=mebibytes * 1024 * 1024)

    lists = candidate_blocks.T
    kinds = relation_offsets.reshape(1, count)
    codes = target_codes.reshape(1, count)

    spread, ranks = pl.pallas_call(
        query_kernel,
        out_shape=(
            jax.ShapeDtypeStruct((owners * 8, count), bf16),
            jax.ShapeDtypeStruct((owners, owners), f32),
        ),
        in_specs=[smem, pl.BlockSpec(memory_space=pltpu.HBM)] + [pl.BlockSpec(memory_space=pltpu.VMEM)] * 5,
        scratch_shapes=[pltpu.VMEM((count, depth), f32), pltpu.SemaphoreType.DMA],
        compiler_params=params(61),
        name="query",
    )(head_offsets, table, relations, kinds, codes, lists, list_lengths)

    held = lax.all_to_all(spread.reshape(owners, 8, count), "entity", 0, 0, tiled=True)

    def pack(*refs):
        pack_kernel(*refs, block_rows)

    packed, targets = pl.pallas_call(
        pack,
        out_shape=(
            jax.ShapeDtypeStruct((owners * 8, HALF * count), bf16),
            jax.ShapeDtypeStruct((16, count), i32),
        ),
        in_specs=[smem] + [pl.BlockSpec(memory_space=pltpu.VMEM)] * 4,
        compiler_params=params(12),
        name="pack",
    )(me, ranks, held.reshape(owners * 8, count), lists, list_lengths)

    received = lax.all_to_all(packed.reshape(owners, 8, HALF * count), "entity", 0, 0, tiled=True)

    rounded = table.astype(bf16)
    query_t, local = pl.pallas_call(
        stats_kernel,
        out_shape=(
            jax.ShapeDtypeStruct((depth, CAP * count), bf16),
            jax.ShapeDtypeStruct((32, count), f32),
        ),
        in_specs=[pl.BlockSpec(memory_space=pltpu.VMEM)] * 3,
        scratch_shapes=[pltpu.VMEM((8, CAP * count), f32)] * 3,
        compiler_params=params(16),
        name="stats",
    )(received.reshape(owners * 8, HALF * count), rounded, targets)

    other = lax.ppermute(local, "entity", [(i, i ^ 1) for i in range(owners)])
    share = pl.pallas_call(
        share_kernel,
        out_shape=jax.ShapeDtypeStruct((owners // 2 * 16, count), f32),
        in_specs=[smem] + [pl.BlockSpec(memory_space=pltpu.VMEM)] * 3,
        compiler_params=params(8),
        name="share",
    )(me, ranks, local, other)
    cores = [[i for i in range(owners) if i % 2 == core] for core in range(2)]
    shared = lax.all_to_all(
        share.reshape(owners // 2, 16, count), "entity", 0, 0, tiled=True, axis_index_groups=cores
    )

    norms, loss = pl.pallas_call(
        merge_kernel,
        out_shape=(jax.ShapeDtypeStruct((16, count), f32), jax.ShapeDtypeStruct((1, count), f32)),
        compiler_params=params(8),
        name="merge",
    )(shared)

    quarter = block_rows // groups

    def grads(which, dtype, norms):
        return pl.pallas_call(
            grads_kernel,
            out_shape=jax.ShapeDtypeStruct((quarter, depth), dtype),
            in_specs=[smem] + [pl.BlockSpec(memory_space=pltpu.VMEM)] * 4,
            scratch_shapes=[pltpu.VMEM((quarter, CAP * count), bf16)],
            compiler_params=params(16),
            cost_estimate=pl.CostEstimate(
                flops=4 * quarter * CAP * count * depth,
                transcendentals=quarter * CAP * count,
                bytes_accessed=4 * quarter * depth + 4 * CAP * count * depth,
            ),
            name="grads",
        )(which.reshape(1), norms, targets, rounded, query_t)

    arrived = []
    for shift in (2, 1, 3):
        part = grads((group + shift) % groups, bf16, norms)
        arrived.append(lax.ppermute(part, "dp", [(i, (i + shift) % groups) for i in range(groups)]))
    last_norms, arrived[0] = lax.optimization_barrier((norms, arrived[0]))
    gradient = grads(group, f32, last_norms)
    for part in arrived:
        gradient = gradient + part.astype(f32)
    return (loss.reshape(count), gradient[None])


def solution(mesh):
    return jax.shard_map(
        per_device,
        mesh=mesh,
        in_specs=(
            P("entity", None, None),
            P("entity", None, None),
            P("dp", None),
            P("dp", None),
            P(("dp", "entity")),
            P(("dp", "entity")),
            P(("dp", "entity")),
        ),
        out_specs=(P(("dp", "entity")), P("entity", "dp", None)),
        check_vma=False,
    )
```

```python
import jax
import jax.numpy as jnp
from jax import lax
from jax.experimental import pallas as pl
from jax.experimental.pallas import tpu as pltpu
from jax.sharding import PartitionSpec as P

f32, bf16, i32 = jnp.float32, jnp.bfloat16, jnp.int32
CAP = 12
PARTS = 8
WIDE = 4
TILE = 1024
CHUNK = 128
NEG = -1e30
HIGH = lax.Precision.HIGHEST


def iota(shape, axis):
    return lax.broadcasted_iota(i32, shape, axis)


def dot(a, b, ca=1, cb=0, precision=None):
    return lax.dot_general(
        a, b, (((ca,), (cb,)), ((), ())), precision=precision, preferred_element_type=f32
    )


def whole(shape):
    return pl.BlockSpec(shape, lambda *_: (0,) * len(shape))


def query_kernel(heads, table, relations, kinds, codes, out, rows, sem):
    count = rows.shape[0]

    def fetch(n, carry):
        pltpu.make_async_copy(
            table.at[pl.ds(heads[n], 1), :], rows.at[pl.ds(n, 1), :], sem
        ).start()
        return carry

    lax.fori_loop(0, count, fetch, 0, unroll=8)
    diagonal = iota((count, count), 0) == iota((count, count), 1)
    kind = jnp.sum(jnp.where(diagonal, kinds[...].astype(f32), 0.0), axis=1, keepdims=True)
    depth = relations.shape[2]
    part = depth // PARTS
    total = PARTS * (part + 8)
    row, column = iota((total, depth), 0), iota((total, depth), 1)
    place = row % (part + 8)
    pick = (place < part) & (row // (part + 8) * part + place == column)
    pick = pick.astype(f32).astype(bf16)
    pltpu.make_async_copy(table.at[pl.ds(0, count), :], rows, sem).wait()
    head = rows[...]
    query = jnp.zeros((count, depth), f32)
    for r in range(relations.shape[0]):
        product = dot(head, relations[r], precision=HIGH)
        query = jnp.where(kind == r, product, query)
    spread = dot(pick, query.astype(bf16), 1, 1)
    place = iota(spread.shape, 0) % (part + 8)
    code = codes[...]
    spread = jnp.where(place == part, (code // 128).astype(f32), spread)
    spread = jnp.where(place == part + 1, (code % 128).astype(f32), spread)
    spread = spread.astype(bf16)
    for z in range(out.shape[0] // total):
        out[z * total : (z + 1) * total, :] = spread


def plan_kernel(me, lists, lengths, ranks, slots, mine):
    sets = lists.shape[1]
    lists_t = lists[...].astype(f32)
    used_t = jnp.where(iota(lists_t.shape, 0) < lengths[...], lists_t, -1.0)
    block = iota((sets, sets), 0).astype(f32)
    listed = jnp.zeros((sets, sets), f32)
    for k in range(lists_t.shape[0]):
        listed = jnp.where(used_t[k : k + 1, :] == block, 1.0, listed)
    before = (iota((sets, sets), 0) < iota((sets, sets), 1)).astype(f32).astype(bf16)
    rank = jnp.where(listed > 0.0, dot(listed.astype(bf16), before), -1.0)
    ranks[...] = rank
    number = iota((sets, sets), 1).astype(f32)
    lane = iota(slots.shape, 1)
    table = jnp.zeros(slots.shape, f32)
    for i in range(CAP):
        held = jnp.sum(jnp.where(rank == float(i), number, 0.0), axis=1, keepdims=True)
        table = jnp.where(lane == i, held, table)
    slots[...] = table.astype(i32)
    own = ranks[pl.ds(me[0], 1), :]
    count = mine.shape[0]
    taken = own == iota((count, sets), 0).astype(f32)
    onehot = taken.astype(f32).astype(bf16)
    width = lists_t.shape[0]
    spread = (iota((width, 128), 0) == iota((width, 128), 1)).astype(f32).astype(bf16)
    padded = dot(lists_t.astype(bf16), spread, 0, 0)
    result = dot(onehot, padded.astype(bf16))
    length = jnp.sum(jnp.where(taken, lengths[...].astype(f32), 0.0), axis=1, keepdims=True)
    used = jnp.sum(taken.astype(f32), axis=1, keepdims=True)
    lane = iota(result.shape, 1)
    result = jnp.where(lane == width, length, result)
    mine[...] = jnp.where(lane == width + 1, used, result)


def pack_kernel(me, slots, held, mine, out, targets, codes, block_rows):
    part = out.shape[0] // PARTS
    stride = part + 8
    first = me[0] // PARTS * PARTS
    for p in range(PARTS):
        for i in range(CAP):
            start = pl.multiple_of(slots[first + p, i] * stride, 8)
            out[p * part : (p + 1) * part, i * 128 : (i + 1) * 128] = held[pl.ds(start, part), :]
    codes[...] = jnp.zeros(codes.shape, f32)
    for i in range(CAP):
        start = pl.multiple_of(slots[me[0], i] * stride + part, 8)
        pair = held[pl.ds(start, 8), :].astype(f32)
        codes[i : i + 1, :] = pair[0:1, :] * 128.0 + pair[1:2, :]
    code = codes[...].astype(i32)
    info = mine[...].astype(i32)
    width = 8
    length = info[:, width : width + 1]
    used = info[:, width + 1 : width + 2] > 0
    entry = code // block_rows
    for _ in range(3):
        entry = jnp.where(entry >= length, entry - length, entry)
    block = jnp.full(code.shape, -1, i32)
    for k in range(width):
        block = jnp.where(entry == k, info[:, k : k + 1], block)
    targets[...] = jnp.where((block == me[0]) & used, code % block_rows, -1)


def stats_kernel(query_t, table, targets, out, top_s, sum_s, tgt_s):
    top_s[...] = jnp.full(top_s.shape, NEG, f32)
    sum_s[...] = jnp.zeros(sum_s.shape, f32)
    tgt_s[...] = jnp.zeros(tgt_s.shape, f32)

    def visit(step, carry):
        rows = table[pl.ds(step * TILE, TILE), :]
        for p in range(CAP // WIDE):
            columns = slice(p * WIDE * 128, (p + 1) * WIDE * 128)
            weights = query_t[:, columns]
            target = slot_lanes(targets, p)
            wanted = target - iota((8, target.shape[1]), 0) - step * TILE
            top, mass, hit = top_s[:, columns], sum_s[:, columns], tgt_s[:, columns]
            for c in range(TILE // CHUNK):
                score = dot(rows[c * CHUNK : (c + 1) * CHUNK, :], weights)
                score = score.reshape(CHUNK // 8, 8, score.shape[1])
                above = jnp.maximum(top, jnp.max(score, axis=0))
                mass = mass * jnp.exp(top - above) + jnp.sum(jnp.exp(score - above[None]), axis=0)
                top = above
                for k in range(CHUNK // 8):
                    hit = jnp.where(wanted == c * CHUNK + k * 8, score[k], hit)
            top_s[:, columns], sum_s[:, columns], tgt_s[:, columns] = top, mass, hit
        return carry

    lax.fori_loop(0, table.shape[0] // TILE, visit, 0)
    top = top_s[...]
    best = jnp.max(top, axis=0, keepdims=True)
    mass = jnp.sum(sum_s[...] * jnp.exp(top - best), axis=0, keepdims=True)
    local = best + jnp.log(mass)
    picked = jnp.sum(tgt_s[...], axis=0, keepdims=True)
    out[...] = jnp.zeros(out.shape, f32)
    for i in range(CAP):
        out[i : i + 1, :] = local[:, i * 128 : (i + 1) * 128]
        out[16 + i : 17 + i, :] = picked[:, i * 128 : (i + 1) * 128]


def slot_lanes(ref, p):
    return jnp.concatenate([ref[i : i + 1, :] for i in range(WIDE * p, WIDE * p + WIDE)], axis=1)


def share_kernel(me, ranks, mine, other, out):
    sets = ranks.shape[0]
    total = out.shape[0]
    core = me[0] % 2
    rank = ranks[...]
    row = iota((total, sets), 0)
    place = row // 16 * 2 + core
    up = (place == iota((total, sets), 1)).astype(f32)
    wide = dot(up.astype(bf16), rank.astype(bf16))
    slot = row % 16
    shared = (wide == slot.astype(f32)) & (slot < CAP)
    shared = shared | (((slot == CAP) | (slot == CAP + 1)) & (up > 0.5))
    shared = shared.astype(f32).astype(bf16)
    slot, source = iota((total, 32), 0) % 16, iota((total, 32), 1)
    keep = (slot == CAP + 1) == (source >= 16)
    wants_target = iota((total, 128), 0) % 16 == CAP + 1

    def rows_of(owner, values):
        owned = ranks[pl.ds(owner, 1), :] == (iota((32, sets), 0) % 16).astype(f32)
        match = jnp.where(keep, dot(shared, owned.astype(f32).astype(bf16), 1, 1), 0.0)
        found = dot(match, values[...], precision=HIGH)
        present = dot(match.astype(bf16), jnp.ones((32, 128), bf16))
        return jnp.where(present > 0.5, found, jnp.where(wants_target, 0.0, NEG))

    first = rows_of(me[0], mine)
    second = rows_of(me[0] + 1 - 2 * core, other)
    best = jnp.maximum(first, second)
    both = best + jnp.log(jnp.exp(first - best) + jnp.exp(second - best))
    out[...] = jnp.where(wants_target, first + second, both)


def merge_kernel(received, norms, loss):
    values = received[...]
    best = jnp.max(values, axis=0)
    mass = jnp.sum(jnp.exp(values - best[None]), axis=0)
    norm = best + jnp.log(mass)
    norms[...] = jnp.where(best <= 0.5 * NEG, -NEG, norm)
    target = jnp.sum(values[:, CAP + 1, :], axis=0, keepdims=True)
    loss[...] = norm[CAP : CAP + 1, :] - target


def grads_kernel(first, norms, targets, table, query_t, early, late, coefficients):
    half = early.shape[0]
    count = 2 * half
    start = pl.multiple_of(first[0] * count, count)
    rows = table[pl.ds(start, count), :]
    for p in range(CAP // WIDE):
        columns = slice(p * WIDE * 128, (p + 1) * WIDE * 128)
        weights = query_t[:, columns]
        norm = slot_lanes(norms, p)
        target = slot_lanes(targets, p)
        wanted = target - iota((8, target.shape[1]), 0) - start
        for c in range(count // CHUNK):
            score = dot(rows[c * CHUNK : (c + 1) * CHUNK, :], weights)
            score = score.reshape(CHUNK // 8, 8, score.shape[1])
            weight = jnp.exp(score - norm[None])
            place = iota(score.shape, 0) * 8 + c * CHUNK
            weight = jnp.where(place == wanted[None], weight - 1.0, weight)
            coefficients[c * CHUNK : (c + 1) * CHUNK, columns] = weight.reshape(CHUNK, -1).astype(bf16)
    early[...] = dot(coefficients[:half, :], query_t[...], 1, 1).astype(early.dtype)
    late[...] = dot(coefficients[half:, :], query_t[...], 1, 1).astype(late.dtype)


def per_device(
    entities,
    relations,
    candidate_blocks,
    list_lengths,
    head_offsets,
    relation_offsets,
    target_codes,
):
    owners = lax.axis_size("entity")
    groups = lax.axis_size("dp")
    table = entities[0]
    block_rows, depth = table.shape
    count = head_offsets.shape[0]
    me = lax.axis_index("entity").astype(i32).reshape(1)
    group = lax.axis_index("dp").astype(i32)
    smem = pl.BlockSpec(memory_space=pltpu.SMEM)

    def params(mebibytes):
        return pltpu.CompilerParams(vmem_limit_bytes=mebibytes * 1024 * 1024)

    lists = candidate_blocks.T
    kinds = relation_offsets.reshape(1, count)
    codes = target_codes.reshape(1, count)

    vmem = pl.BlockSpec(memory_space=pltpu.VMEM)
    stride = depth // PARTS + 8
    spread = pl.pallas_call(
        query_kernel,
        out_shape=jax.ShapeDtypeStruct((owners * stride, count), bf16),
        in_specs=[smem, pl.BlockSpec(memory_space=pltpu.HBM)] + [vmem] * 3,
        scratch_shapes=[pltpu.VMEM((count, depth), f32), pltpu.SemaphoreType.DMA],
        compiler_params=params(61),
        name="query",
    )(head_offsets, table, relations, kinds, codes)
    held = lax.all_to_all(spread.reshape(owners, stride, count), "entity", 0, 0, tiled=True)

    ranks, slots, mine = pl.pallas_call(
        plan_kernel,
        out_shape=(
            jax.ShapeDtypeStruct((owners, owners), f32),
            jax.ShapeDtypeStruct((owners, 128), i32),
            jax.ShapeDtypeStruct((16, 128), f32),
        ),
        in_specs=[smem] + [vmem] * 2,
        compiler_params=params(8),
        name="plan",
    )(me, lists, list_lengths)

    def pack(*refs):
        pack_kernel(*refs, block_rows)

    packed, targets = pl.pallas_call(
        pack,
        out_shape=(
            jax.ShapeDtypeStruct((depth, CAP * count), bf16),
            jax.ShapeDtypeStruct((16, count), i32),
        ),
        in_specs=[smem, smem] + [vmem] * 2,
        scratch_shapes=[pltpu.VMEM((16, count), f32)],
        compiler_params=params(8),
        name="pack",
    )(me, slots, held.reshape(owners * stride, count), mine)
    planes = [[z * PARTS + p for p in range(PARTS)] for z in range(owners // PARTS)]
    query_t = lax.all_to_all(
        packed.reshape(PARTS, depth // PARTS, CAP * count),
        "entity",
        0,
        0,
        tiled=True,
        axis_index_groups=planes,
    ).reshape(depth, CAP * count)

    rounded = table.astype(bf16)
    local = pl.pallas_call(
        stats_kernel,
        out_shape=jax.ShapeDtypeStruct((32, count), f32),
        in_specs=[vmem] * 3,
        scratch_shapes=[pltpu.VMEM((8, CAP * count), f32)] * 3,
        compiler_params=params(16),
        name="stats",
    )(query_t, rounded, targets)

    other = lax.ppermute(local, "entity", [(i, i ^ 1) for i in range(owners)])
    share = pl.pallas_call(
        share_kernel,
        out_shape=jax.ShapeDtypeStruct((owners // 2 * 16, count), f32),
        in_specs=[smem] + [vmem] * 3,
        compiler_params=params(8),
        name="share",
    )(me, ranks, local, other)
    cores = [[i for i in range(owners) if i % 2 == core] for core in range(2)]
    shared = lax.all_to_all(
        share.reshape(owners // 2, 16, count), "entity", 0, 0, tiled=True, axis_index_groups=cores
    )

    norms, loss = pl.pallas_call(
        merge_kernel,
        out_shape=(jax.ShapeDtypeStruct((16, count), f32), jax.ShapeDtypeStruct((1, count), f32)),
        compiler_params=params(8),
        name="merge",
    )(shared)

    quarter = block_rows // groups

    def grads(which, early, late):
        return pl.pallas_call(
            grads_kernel,
            out_shape=(
                jax.ShapeDtypeStruct((quarter // 2, depth), early),
                jax.ShapeDtypeStruct((quarter // 2, depth), late),
            ),
            in_specs=[smem] + [vmem] * 4,
            scratch_shapes=[pltpu.VMEM((quarter, CAP * count), bf16)],
            compiler_params=params(16),
            cost_estimate=pl.CostEstimate(
                flops=4 * quarter * CAP * count * depth,
                transcendentals=quarter * CAP * count,
                bytes_accessed=4 * quarter * depth + 4 * CAP * count * depth,
            ),
            name="grads",
        )((which % groups).reshape(1), norms, targets, rounded, query_t)

    assert groups == 4

    def up(value):
        return lax.ppermute(value, "dp", [(i, (i + 1) % groups) for i in range(groups)])

    def down(value):
        return lax.ppermute(value, "dp", [(i, (i - 1) % groups) for i in range(groups)])

    far_early, far_late = grads(group + 2, bf16, bf16)
    relay_early, relay_late = up(far_early), down(far_late)
    next_early, next_late = grads(group + 1, f32, bf16)
    last_early, last_late = grads(group + 3, bf16, f32)
    from_below_late, from_above_early = up(next_late), down(last_early)
    own_early, own_late = grads(group, f32, f32)
    from_below_early = up((next_early + relay_early.astype(f32)).astype(bf16))
    from_above_late = down((last_late + relay_late.astype(f32)).astype(bf16))
    early = own_early + from_above_early.astype(f32) + from_below_early.astype(f32)
    late = own_late + from_below_late.astype(f32) + from_above_late.astype(f32)
    gradient = jnp.concatenate([early, late], axis=0)
    return (loss.reshape(count), gradient[None])


def solution(mesh):
    return jax.shard_map(
        per_device,
        mesh=mesh,
        in_specs=(
            P("entity", None, None),
            P("entity", None, None),
            P("dp", None),
            P("dp", None),
            P(("dp", "entity")),
            P(("dp", "entity")),
            P(("dp", "entity")),
        ),
        out_specs=(P(("dp", "entity")), P("entity", "dp", None)),
        check_vma=False,
    )
```

```python
import jax
import jax.numpy as jnp
from jax import lax
from jax.experimental import pallas as pl
from jax.experimental.pallas import tpu as pltpu
from jax.sharding import PartitionSpec as P

f32, bf16, i32 = jnp.float32, jnp.bfloat16, jnp.int32
CAP = 12
PARTS = 16
WIDE = 4
TILE = 1024
CHUNK = 128
NEG = -1e30
NONE_ROW = 14
HIGH = lax.Precision.HIGHEST


def iota(shape, axis):
    return lax.broadcasted_iota(i32, shape, axis)


def dot(a, b, ca=1, cb=0, precision=None):
    return lax.dot_general(
        a, b, (((ca,), (cb,)), ((), ())), precision=precision, preferred_element_type=f32
    )


def whole(shape):
    return pl.BlockSpec(shape, lambda *_: (0,) * len(shape))


def query_kernel(heads, table, operators, kinds, codes, out, rows, relations, sem, other_sem):
    count = rows.shape[0]
    load = pltpu.make_async_copy(operators, relations, other_sem)
    load.start()

    def fetch(n, carry):
        pltpu.make_async_copy(
            table.at[pl.ds(heads[n], 1), :], rows.at[pl.ds(n, 1), :], sem
        ).start()
        return carry

    lax.fori_loop(0, count, fetch, 0, unroll=8)
    diagonal = iota((count, count), 0) == iota((count, count), 1)
    kind = jnp.sum(jnp.where(diagonal, kinds[...].astype(f32), 0.0), axis=1, keepdims=True)
    depth = relations.shape[2]
    part = depth // PARTS
    total = PARTS * (part + 8)
    row, column = iota((total, depth), 0), iota((total, depth), 1)
    place = row % (part + 8)
    pick = (place < part) & (row // (part + 8) * part + place == column)
    pick = pick.astype(f32).astype(bf16)
    load.wait()
    pltpu.make_async_copy(table.at[pl.ds(0, count), :], rows, sem).wait()
    head = rows[...]
    query = jnp.zeros((count, depth), f32)
    for r in range(relations.shape[0]):
        product = dot(head, relations[r], precision=HIGH)
        query = jnp.where(kind == r, product, query)
    spread = dot(pick, query.astype(bf16), 1, 1)
    place = iota(spread.shape, 0) % (part + 8)
    code = codes[...]
    spread = jnp.where(place == part, (code // 128).astype(f32), spread)
    spread = jnp.where(place == part + 1, (code % 128).astype(f32), spread)
    spread = spread.astype(bf16)
    for z in range(out.shape[0] // total):
        out[z * total : (z + 1) * total, :] = spread


def plan_kernel(me, lists, lengths, slots, mine, matches, ranks):
    sets = lists.shape[1]
    lists_t = lists[...].astype(f32)
    used_t = jnp.where(iota(lists_t.shape, 0) < lengths[...], lists_t, -1.0)
    block = iota((sets, sets), 0).astype(f32)
    listed = jnp.zeros((sets, sets), f32)
    for k in range(lists_t.shape[0]):
        listed = jnp.where(used_t[k : k + 1, :] == block, 1.0, listed)
    before = (iota((sets, sets), 0) < iota((sets, sets), 1)).astype(f32).astype(bf16)
    rank = jnp.where(listed > 0.0, dot(listed.astype(bf16), before), -1.0)
    ranks[...] = rank
    group = ranks[pl.ds(pl.multiple_of(me[0] // PARTS * PARTS, PARTS), PARTS), :]
    number = iota(group.shape, 1).astype(f32)
    lane = iota(slots.shape, 1)
    table = jnp.zeros(slots.shape, f32)
    for i in range(CAP):
        held = jnp.sum(jnp.where(group == float(i), number, 0.0), axis=1, keepdims=True)
        table = jnp.where(lane == i, held, table)
    slots[...] = table.astype(i32)
    own = ranks[pl.ds(me[0], 1), :]
    count = mine.shape[0]
    taken = own == iota((count, sets), 0).astype(f32)
    onehot = taken.astype(f32).astype(bf16)
    width = lists_t.shape[0]
    spread = (iota((width, 128), 0) == iota((width, 128), 1)).astype(f32).astype(bf16)
    padded = dot(lists_t.astype(bf16), spread, 0, 0)
    result = dot(onehot, padded.astype(bf16))
    length = jnp.sum(jnp.where(taken, lengths[...].astype(f32), 0.0), axis=1, keepdims=True)
    used = jnp.sum(taken.astype(f32), axis=1, keepdims=True)
    lane = iota(result.shape, 1)
    result = jnp.where(lane == width, length, result)
    mine[...] = jnp.where(lane == width + 1, used, result)
    total = matches.shape[1]
    core = me[0] % 2
    row = iota((total, sets), 0)
    up = (row // 16 * 2 + core == iota((total, sets), 1)).astype(f32)
    wide = dot(up.astype(bf16), rank.astype(bf16))
    slot = row % 16
    shared = (wide == slot.astype(f32)) & (slot < CAP)
    shared = shared | (((slot == CAP) | (slot == CAP + 1)) & (up > 0.5))
    shared = shared.astype(f32).astype(bf16)
    slot, source = iota((total, 32), 0) % 16, iota((total, 32), 1)
    keep = (slot == CAP + 1) == (source >= 16)
    for which, owner in enumerate((me[0], me[0] + 1 - 2 * core)):
        owned = ranks[pl.ds(owner, 1), :] == (iota((32, sets), 0) % 16).astype(f32)
        match = jnp.where(keep, dot(shared, owned.astype(f32).astype(bf16), 1, 1), 0.0)
        found = jnp.sum(match, axis=1, keepdims=True) > 0.5
        nothing = (source == NONE_ROW) & (slot != CAP + 1) & jnp.logical_not(found)
        matches[which] = jnp.where(nothing, 1.0, match)


def pack_kernel(me, slots, held, mine, out, targets, codes, block_rows):
    part = out.shape[0] // PARTS
    stride = part + 8
    for p in range(PARTS):
        for i in range(CAP):
            start = pl.multiple_of(slots[p, i] * stride, 8)
            out[p * part : (p + 1) * part, i * 128 : (i + 1) * 128] = held[pl.ds(start, part), :]
    codes[...] = jnp.zeros(codes.shape, f32)
    for i in range(CAP):
        start = pl.multiple_of(slots[me[0] % PARTS, i] * stride + part, 8)
        pair = held[pl.ds(start, 8), :].astype(f32)
        codes[i : i + 1, :] = pair[0:1, :] * 128.0 + pair[1:2, :]
    code = codes[...].astype(i32)
    info = mine[...].astype(i32)
    width = 8
    length = info[:, width : width + 1]
    used = info[:, width + 1 : width + 2] > 0
    entry = code // block_rows
    for _ in range(3):
        entry = jnp.where(entry >= length, entry - length, entry)
    block = jnp.full(code.shape, -1, i32)
    for k in range(width):
        block = jnp.where(entry == k, info[:, k : k + 1], block)
    targets[...] = jnp.where((block == me[0]) & used, code % block_rows, -1)


def stats_kernel(query_t, table, targets, out, top_s, sum_s, tgt_s):
    top_s[...] = jnp.full(top_s.shape, NEG, f32)
    sum_s[...] = jnp.zeros(sum_s.shape, f32)
    tgt_s[...] = jnp.zeros(tgt_s.shape, f32)

    def visit(step, carry):
        rows = table[pl.ds(step * TILE, TILE), :]
        for p in range(CAP // WIDE):
            columns = slice(p * WIDE * 128, (p + 1) * WIDE * 128)
            weights = query_t[:, columns]
            target = slot_lanes(targets, p)
            wanted = target - iota((8, target.shape[1]), 0) - step * TILE
            top, mass, hit = top_s[:, columns], sum_s[:, columns], tgt_s[:, columns]
            for c in range(TILE // CHUNK):
                score = dot(rows[c * CHUNK : (c + 1) * CHUNK, :], weights)
                score = score.reshape(CHUNK // 8, 8, score.shape[1])
                above = jnp.maximum(top, jnp.max(score, axis=0))
                mass = mass * jnp.exp(top - above) + jnp.sum(jnp.exp(score - above[None]), axis=0)
                top = above
                for k in range(CHUNK // 8):
                    hit = jnp.where(wanted == c * CHUNK + k * 8, score[k], hit)
            top_s[:, columns], sum_s[:, columns], tgt_s[:, columns] = top, mass, hit
        return carry

    lax.fori_loop(0, table.shape[0] // TILE, visit, 0)
    top = top_s[...]
    best = jnp.max(top, axis=0, keepdims=True)
    mass = jnp.sum(sum_s[...] * jnp.exp(top - best), axis=0, keepdims=True)
    local = best + jnp.log(mass)
    picked = jnp.sum(tgt_s[...], axis=0, keepdims=True)
    out[...] = jnp.where(iota(out.shape, 0) == NONE_ROW, NEG, 0.0)
    for i in range(CAP):
        out[i : i + 1, :] = local[:, i * 128 : (i + 1) * 128]
        out[16 + i : 17 + i, :] = picked[:, i * 128 : (i + 1) * 128]


def slot_lanes(ref, p):
    return jnp.concatenate([ref[i : i + 1, :] for i in range(WIDE * p, WIDE * p + WIDE)], axis=1)


def share_kernel(matches, mine, other, out):
    wants_target = iota(out.shape, 0) % 16 == CAP + 1
    first = dot(matches[0], mine[...], precision=HIGH)
    second = dot(matches[1], other[...], precision=HIGH)
    best = jnp.maximum(first, second)
    both = best + jnp.log(jnp.exp(first - best) + jnp.exp(second - best))
    out[...] = jnp.where(wants_target, first + second, both)


def merge_kernel(received, norms, loss):
    values = received[...]
    best = jnp.max(values, axis=0)
    mass = jnp.sum(jnp.exp(values - best[None]), axis=0)
    norm = best + jnp.log(mass)
    norms[...] = jnp.where(best <= 0.5 * NEG, -NEG, norm)
    target = jnp.sum(values[:, CAP + 1, :], axis=0, keepdims=True)
    loss[...] = norm[CAP : CAP + 1, :] - target


def grads_kernel(first, norms, targets, table, query_t, early, late, coefficients):
    half = early.shape[0]
    count = 2 * half
    start = pl.multiple_of(first[0] * count, count)
    rows = table[pl.ds(start, count), :]
    for p in range(CAP // WIDE):
        columns = slice(p * WIDE * 128, (p + 1) * WIDE * 128)
        weights = query_t[:, columns]
        norm = slot_lanes(norms, p)
        target = slot_lanes(targets, p)
        wanted = target - iota((8, target.shape[1]), 0) - start
        for c in range(count // CHUNK):
            score = dot(rows[c * CHUNK : (c + 1) * CHUNK, :], weights)
            score = score.reshape(CHUNK // 8, 8, score.shape[1])
            weight = jnp.exp(score - norm[None])
            place = iota(score.shape, 0) * 8 + c * CHUNK
            weight = jnp.where(place == wanted[None], weight - 1.0, weight)
            coefficients[c * CHUNK : (c + 1) * CHUNK, columns] = weight.reshape(CHUNK, -1).astype(bf16)
    early[...] = dot(coefficients[:half, :], query_t[...], 1, 1).astype(early.dtype)
    late[...] = dot(coefficients[half:, :], query_t[...], 1, 1).astype(late.dtype)


def per_device(
    entities,
    relations,
    candidate_blocks,
    list_lengths,
    head_offsets,
    relation_offsets,
    target_codes,
):
    owners = lax.axis_size("entity")
    groups = lax.axis_size("dp")
    table = entities[0]
    block_rows, depth = table.shape
    count = head_offsets.shape[0]
    me = lax.axis_index("entity").astype(i32).reshape(1)
    group = lax.axis_index("dp").astype(i32)
    smem = pl.BlockSpec(memory_space=pltpu.SMEM)

    def params(mebibytes):
        return pltpu.CompilerParams(vmem_limit_bytes=mebibytes * 1024 * 1024)

    lists = candidate_blocks.T
    kinds = relation_offsets.reshape(1, count)
    codes = target_codes.reshape(1, count)

    vmem = pl.BlockSpec(memory_space=pltpu.VMEM)
    stride = depth // PARTS + 8
    spread = pl.pallas_call(
        query_kernel,
        out_shape=jax.ShapeDtypeStruct((owners * stride, count), bf16),
        in_specs=[smem] + [pl.BlockSpec(memory_space=pltpu.HBM)] * 2 + [vmem] * 2,
        scratch_shapes=[
            pltpu.VMEM((count, depth), f32),
            pltpu.VMEM(relations.shape, f32),
            pltpu.SemaphoreType.DMA,
            pltpu.SemaphoreType.DMA,
        ],
        compiler_params=params(61),
        name="query",
    )(head_offsets, table, relations, kinds, codes)
    held = lax.all_to_all(spread.reshape(owners, stride, count), "entity", 0, 0, tiled=True)

    share_rows = owners // 2 * 16
    slots, mine, matches = pl.pallas_call(
        plan_kernel,
        out_shape=(
            jax.ShapeDtypeStruct((PARTS, 128), i32),
            jax.ShapeDtypeStruct((16, 128), f32),
            jax.ShapeDtypeStruct((2, share_rows, 32), f32),
        ),
        in_specs=[smem] + [vmem] * 2,
        scratch_shapes=[pltpu.VMEM((owners, owners), f32)],
        compiler_params=params(8),
        name="plan",
    )(me, lists, list_lengths)

    def pack(*refs):
        pack_kernel(*refs, block_rows)

    packed, targets = pl.pallas_call(
        pack,
        out_shape=(
            jax.ShapeDtypeStruct((depth, CAP * count), bf16),
            jax.ShapeDtypeStruct((16, count), i32),
        ),
        in_specs=[smem, smem] + [vmem] * 2,
        scratch_shapes=[pltpu.VMEM((16, count), f32)],
        compiler_params=params(8),
        name="pack",
    )(me, slots, held.reshape(owners * stride, count), mine)
    planes = [[z * PARTS + p for p in range(PARTS)] for z in range(owners // PARTS)]
    query_t = lax.all_to_all(
        packed.reshape(PARTS, depth // PARTS, CAP * count),
        "entity",
        0,
        0,
        tiled=True,
        axis_index_groups=planes,
    ).reshape(depth, CAP * count)

    rounded = table.astype(bf16)
    local = pl.pallas_call(
        stats_kernel,
        out_shape=jax.ShapeDtypeStruct((32, count), f32),
        in_specs=[vmem] * 3,
        scratch_shapes=[pltpu.VMEM((8, CAP * count), f32)] * 3,
        compiler_params=params(16),
        name="stats",
    )(query_t, rounded, targets)

    other = lax.ppermute(local, "entity", [(i, i ^ 1) for i in range(owners)])
    share = pl.pallas_call(
        share_kernel,
        out_shape=jax.ShapeDtypeStruct((share_rows, count), f32),
        in_specs=[vmem] * 3,
        compiler_params=params(8),
        name="share",
    )(matches, local, other)
    cores = [[i for i in range(owners) if i % 2 == core] for core in range(2)]
    shared = lax.all_to_all(
        share.reshape(owners // 2, 16, count), "entity", 0, 0, tiled=True, axis_index_groups=cores
    )

    norms, loss = pl.pallas_call(
        merge_kernel,
        out_shape=(jax.ShapeDtypeStruct((16, count), f32), jax.ShapeDtypeStruct((1, count), f32)),
        compiler_params=params(8),
        name="merge",
    )(shared)

    quarter = block_rows // groups

    def grads(which, early, late, norms=norms):
        return pl.pallas_call(
            grads_kernel,
            out_shape=(
                jax.ShapeDtypeStruct((quarter // 2, depth), early),
                jax.ShapeDtypeStruct((quarter // 2, depth), late),
            ),
            in_specs=[smem] + [vmem] * 4,
            scratch_shapes=[pltpu.VMEM((quarter, CAP * count), bf16)],
            compiler_params=params(16),
            cost_estimate=pl.CostEstimate(
                flops=4 * quarter * CAP * count * depth,
                transcendentals=quarter * CAP * count,
                bytes_accessed=4 * quarter * depth + 4 * CAP * count * depth,
            ),
            name="grads",
        )((which % groups).reshape(1), norms, targets, rounded, query_t)

    assert groups == 4

    def up(value):
        return lax.ppermute(value, "dp", [(i, (i + 1) % groups) for i in range(groups)])

    def down(value):
        return lax.ppermute(value, "dp", [(i, (i - 1) % groups) for i in range(groups)])

    far_early, far_late = grads(group + 2, bf16, bf16)
    relay_early, relay_late = up(far_early), down(far_late)
    next_early, next_late = grads(group + 1, f32, bf16)
    last_early, last_late = grads(group + 3, bf16, f32)
    from_below_late, from_above_early = up(next_late), down(last_early)
    next_early = (next_early + relay_early.astype(f32)).astype(bf16)
    last_late = (last_late + relay_late.astype(f32)).astype(bf16)
    from_below_early, from_above_late = up(next_early), down(last_late)
    own_norms, next_early, last_late = lax.optimization_barrier((norms, next_early, last_late))
    own_early, own_late = grads(group, f32, f32, own_norms)
    early = own_early + from_above_early.astype(f32) + from_below_early.astype(f32)
    late = own_late + from_below_late.astype(f32) + from_above_late.astype(f32)
    gradient = jnp.concatenate([early, late], axis=0)
    return (loss.reshape(count), gradient[None])


def solution(mesh):
    return jax.shard_map(
        per_device,
        mesh=mesh,
        in_specs=(
            P("entity", None, None),
            P("entity", None, None),
            P("dp", None),
            P("dp", None),
            P(("dp", "entity")),
            P(("dp", "entity")),
            P(("dp", "entity")),
        ),
        out_specs=(P(("dp", "entity")), P("entity", "dp", None)),
        check_vma=False,
    )
```

```python
import jax
import jax.numpy as jnp
from jax import lax
from jax.experimental import pallas as pl
from jax.experimental.pallas import tpu as pltpu
from jax.sharding import PartitionSpec as P

f32, bf16, i32 = jnp.float32, jnp.bfloat16, jnp.int32
CAP = 12
PARTS = 16
WIDE = 4
TILE = 1024
CHUNK = 128
NEG = -1e30
NONE_ROW = 14
HIGH = lax.Precision.HIGHEST


def iota(shape, axis):
    return lax.broadcasted_iota(i32, shape, axis)


def dot(a, b, ca=1, cb=0, precision=None):
    return lax.dot_general(
        a, b, (((ca,), (cb,)), ((), ())), precision=precision, preferred_element_type=f32
    )


def whole(shape):
    return pl.BlockSpec(shape, lambda *_: (0,) * len(shape))


def query_kernel(heads, table, operators, kinds, codes, out, rows, relations, sem, other_sem):
    count = rows.shape[0]
    load = pltpu.make_async_copy(operators, relations, other_sem)
    load.start()

    def fetch(n, carry):
        pltpu.make_async_copy(
            table.at[pl.ds(heads[n], 1), :], rows.at[pl.ds(n, 1), :], sem
        ).start()
        return carry

    lax.fori_loop(0, count, fetch, 0, unroll=8)
    diagonal = iota((count, count), 0) == iota((count, count), 1)
    kind = jnp.sum(jnp.where(diagonal, kinds[...].astype(f32), 0.0), axis=1, keepdims=True)
    depth = relations.shape[2]
    part = depth // PARTS
    total = PARTS * (part + 8)
    row, column = iota((total, depth), 0), iota((total, depth), 1)
    place = row % (part + 8)
    pick = (place < part) & (row // (part + 8) * part + place == column)
    pick = pick.astype(f32).astype(bf16)
    load.wait()
    pltpu.make_async_copy(table.at[pl.ds(0, count), :], rows, sem).wait()
    head = rows[...]
    query = jnp.zeros((count, depth), f32)
    for r in range(relations.shape[0]):
        product = dot(head, relations[r], precision=HIGH)
        query = jnp.where(kind == r, product, query)
    spread = dot(pick, query.astype(bf16), 1, 1)
    place = iota(spread.shape, 0) % (part + 8)
    code = codes[...]
    spread = jnp.where(place == part, (code // 128).astype(f32), spread)
    spread = jnp.where(place == part + 1, (code % 128).astype(f32), spread)
    spread = spread.astype(bf16)
    for z in range(out.shape[0] // total):
        out[z * total : (z + 1) * total, :] = spread


def plan_kernel(me, lists, lengths, slots, mine, matches, ranks):
    sets = lists.shape[1]
    lists_t = lists[...].astype(f32)
    used_t = jnp.where(iota(lists_t.shape, 0) < lengths[...], lists_t, -1.0)
    block = iota((sets, sets), 0).astype(f32)
    listed = jnp.zeros((sets, sets), f32)
    for k in range(lists_t.shape[0]):
        listed = jnp.where(used_t[k : k + 1, :] == block, 1.0, listed)
    before = (iota((sets, sets), 0) < iota((sets, sets), 1)).astype(f32).astype(bf16)
    rank = jnp.where(listed > 0.0, dot(listed.astype(bf16), before), -1.0)
    ranks[...] = rank
    group = ranks[pl.ds(pl.multiple_of(me[0] // PARTS * PARTS, PARTS), PARTS), :]
    number = iota(group.shape, 1).astype(f32)
    lane = iota(slots.shape, 1)
    table = jnp.zeros(slots.shape, f32)
    for i in range(CAP):
        held = jnp.sum(jnp.where(group == float(i), number, 0.0), axis=1, keepdims=True)
        table = jnp.where(lane == i, held, table)
    slots[...] = table.astype(i32)
    own = ranks[pl.ds(me[0], 1), :]
    count = mine.shape[0]
    taken = own == iota((count, sets), 0).astype(f32)
    onehot = taken.astype(f32).astype(bf16)
    width = lists_t.shape[0]
    spread = (iota((width, 128), 0) == iota((width, 128), 1)).astype(f32).astype(bf16)
    padded = dot(lists_t.astype(bf16), spread, 0, 0)
    result = dot(onehot, padded.astype(bf16))
    length = jnp.sum(jnp.where(taken, lengths[...].astype(f32), 0.0), axis=1, keepdims=True)
    used = jnp.sum(taken.astype(f32), axis=1, keepdims=True)
    lane = iota(result.shape, 1)
    result = jnp.where(lane == width, length, result)
    mine[...] = jnp.where(lane == width + 1, used, result)
    total = matches.shape[1]
    core = me[0] % 2
    row = iota((total, sets), 0)
    up = (row // 16 * 2 + core == iota((total, sets), 1)).astype(f32)
    wide = dot(up.astype(bf16), rank.astype(bf16))
    slot = row % 16
    shared = (wide == slot.astype(f32)) & (slot < CAP)
    shared = shared | (((slot == CAP) | (slot == CAP + 1)) & (up > 0.5))
    shared = shared.astype(f32).astype(bf16)
    slot, source = iota((total, 32), 0) % 16, iota((total, 32), 1)
    keep = (slot == CAP + 1) == (source >= 16)
    for which, owner in enumerate((me[0], me[0] + 1 - 2 * core)):
        owned = ranks[pl.ds(owner, 1), :] == (iota((32, sets), 0) % 16).astype(f32)
        match = jnp.where(keep, dot(shared, owned.astype(f32).astype(bf16), 1, 1), 0.0)
        found = jnp.sum(match, axis=1, keepdims=True) > 0.5
        nothing = (source == NONE_ROW) & (slot != CAP + 1) & jnp.logical_not(found)
        matches[which] = jnp.where(nothing, 1.0, match)


def pack_kernel(me, slots, held, mine, out, targets, codes, block_rows):
    part = out.shape[0] // PARTS
    stride = part + 8
    for p in range(PARTS):
        for i in range(CAP):
            start = pl.multiple_of(slots[p, i] * stride, 8)
            out[p * part : (p + 1) * part, i * 128 : (i + 1) * 128] = held[pl.ds(start, part), :]
    codes[...] = jnp.zeros(codes.shape, f32)
    for i in range(CAP):
        start = pl.multiple_of(slots[me[0] % PARTS, i] * stride + part, 8)
        pair = held[pl.ds(start, 8), :].astype(f32)
        codes[i : i + 1, :] = pair[0:1, :] * 128.0 + pair[1:2, :]
    code = codes[...].astype(i32)
    info = mine[...].astype(i32)
    width = 8
    length = info[:, width : width + 1]
    used = info[:, width + 1 : width + 2] > 0
    entry = code // block_rows
    for _ in range(3):
        entry = jnp.where(entry >= length, entry - length, entry)
    block = jnp.full(code.shape, -1, i32)
    for k in range(width):
        block = jnp.where(entry == k, info[:, k : k + 1], block)
    targets[...] = jnp.where((block == me[0]) & used, code % block_rows, -1)


def stats_kernel(query_t, table, targets, out, top_s, sum_s, tgt_s):
    top_s[...] = jnp.full(top_s.shape, NEG, f32)
    sum_s[...] = jnp.zeros(sum_s.shape, f32)
    tgt_s[...] = jnp.zeros(tgt_s.shape, f32)

    def visit(step, carry):
        rows = table[pl.ds(step * TILE, TILE), :]
        for p in range(CAP // WIDE):
            columns = slice(p * WIDE * 128, (p + 1) * WIDE * 128)
            weights = query_t[:, columns]
            target = slot_lanes(targets, p)
            wanted = target - iota((8, target.shape[1]), 0) - step * TILE
            top, mass, hit = top_s[:, columns], sum_s[:, columns], tgt_s[:, columns]
            for c in range(TILE // CHUNK):
                score = dot(rows[c * CHUNK : (c + 1) * CHUNK, :], weights)
                score = score.reshape(CHUNK // 8, 8, score.shape[1])
                above = jnp.maximum(top, jnp.max(score, axis=0))
                mass = mass * jnp.exp(top - above) + jnp.sum(jnp.exp(score - above[None]), axis=0)
                top = above
                for k in range(CHUNK // 8):
                    hit = jnp.where(wanted == c * CHUNK + k * 8, score[k], hit)
            top_s[:, columns], sum_s[:, columns], tgt_s[:, columns] = top, mass, hit
        return carry

    lax.fori_loop(0, table.shape[0] // TILE, visit, 0)
    top = top_s[...]
    best = jnp.max(top, axis=0, keepdims=True)
    mass = jnp.sum(sum_s[...] * jnp.exp(top - best), axis=0, keepdims=True)
    local = best + jnp.log(mass)
    picked = jnp.sum(tgt_s[...], axis=0, keepdims=True)
    out[...] = jnp.where(iota(out.shape, 0) == NONE_ROW, NEG, 0.0)
    for i in range(CAP):
        out[i : i + 1, :] = local[:, i * 128 : (i + 1) * 128]
        out[16 + i : 17 + i, :] = picked[:, i * 128 : (i + 1) * 128]


def slot_lanes(ref, p, base=0):
    first = base + WIDE * p
    return jnp.concatenate([ref[i : i + 1, :] for i in range(first, first + WIDE)], axis=1)


def share_kernel(matches, mine, other, out):
    wants_target = iota(out.shape, 0) % 16 == CAP + 1
    first = dot(matches[0], mine[...], precision=HIGH)
    second = dot(matches[1], other[...], precision=HIGH)
    best = jnp.maximum(first, second)
    both = best + jnp.log(jnp.exp(first - best) + jnp.exp(second - best))
    out[...] = jnp.where(wants_target, first + second, both)


def merge_kernel(received, targets, info, loss):
    values = received[...]
    best = jnp.max(values, axis=0)
    mass = jnp.sum(jnp.exp(values - best[None]), axis=0)
    norm = best + jnp.log(mass)
    info[0:16, :] = jnp.where(best <= 0.5 * NEG, -NEG, norm)
    info[16:32, :] = targets[...].astype(f32)
    target = jnp.sum(values[:, CAP + 1, :], axis=0, keepdims=True)
    loss[...] = norm[CAP : CAP + 1, :] - target


def rows_gradient(start, rows, info, query_t, coefficients):
    count = rows.shape[0]
    for p in range(CAP // WIDE):
        columns = slice(p * WIDE * 128, (p + 1) * WIDE * 128)
        weights = query_t[:, columns]
        norm = slot_lanes(info, p)
        target = slot_lanes(info, p, 16).astype(i32)
        wanted = target - iota((8, target.shape[1]), 0) - start
        for c in range(count // CHUNK):
            score = dot(rows[c * CHUNK : (c + 1) * CHUNK, :], weights)
            score = score.reshape(CHUNK // 8, 8, score.shape[1])
            weight = jnp.exp(score - norm[None])
            place = iota(score.shape, 0) * 8 + c * CHUNK
            weight = jnp.where(place == wanted[None], weight - 1.0, weight)
            coefficients[c * CHUNK : (c + 1) * CHUNK, columns] = weight.reshape(CHUNK, -1).astype(bf16)
    return dot(coefficients[...], query_t[...], 1, 1)


def own_kernel(group, info, table, query_t, out, coefficients):
    half = coefficients.shape[0]
    for h in range(out.shape[0] // half):
        start = pl.multiple_of(group[0] * out.shape[0] + h * half, half)
        rows = table[pl.ds(start, half), :]
        out[h * half : (h + 1) * half, :] = rows_gradient(start, rows, info, query_t, coefficients)


def rest_kernel(
    group, infos, table, own, next_t, last_t, far_t, out, total, queries, coefficients, load_sems, own_sem, sems
):
    half = coefficients.shape[0]
    groups = infos.shape[0]
    loads = [
        pltpu.make_async_copy(query_t, queries.at[i], load_sems.at[i])
        for i, query_t in enumerate((next_t, last_t, far_t))
    ]
    for load in loads:
        load.start()
    own_load = pltpu.make_async_copy(own, total, own_sem)
    own_load.start()
    copies = []
    for h in range(out.shape[0] // half):
        start = pl.multiple_of(group[0] * out.shape[0] + h * half, half)
        rows = table[pl.ds(start, half), :]
        here = slice(h * half, (h + 1) * half)
        gradient = jnp.zeros((half, out.shape[1]), f32)
        for i, shift in enumerate((1, 3, 2)):
            if h == 0:
                loads[i].wait()
            info = infos.at[(group[0] + shift) % groups]
            gradient = gradient + rows_gradient(start, rows, info, queries.at[i], coefficients)
        if h == 0:
            own_load.wait()
        total[here, :] = total[here, :] + gradient
        copies.append(pltpu.make_async_copy(total.at[here, :], out.at[here, :], sems.at[h]))
        copies[-1].start()
    for copy in copies:
        copy.wait()


def per_device(
    entities,
    relations,
    candidate_blocks,
    list_lengths,
    head_offsets,
    relation_offsets,
    target_codes,
):
    owners = lax.axis_size("entity")
    groups = lax.axis_size("dp")
    table = entities[0]
    block_rows, depth = table.shape
    count = head_offsets.shape[0]
    me = lax.axis_index("entity").astype(i32).reshape(1)
    group = lax.axis_index("dp").astype(i32)
    smem = pl.BlockSpec(memory_space=pltpu.SMEM)

    def params(mebibytes):
        return pltpu.CompilerParams(vmem_limit_bytes=mebibytes * 1024 * 1024)

    lists = candidate_blocks.T
    kinds = relation_offsets.reshape(1, count)
    codes = target_codes.reshape(1, count)

    vmem = pl.BlockSpec(memory_space=pltpu.VMEM)
    stride = depth // PARTS + 8
    spread = pl.pallas_call(
        query_kernel,
        out_shape=jax.ShapeDtypeStruct((owners * stride, count), bf16),
        in_specs=[smem] + [pl.BlockSpec(memory_space=pltpu.HBM)] * 2 + [vmem] * 2,
        scratch_shapes=[
            pltpu.VMEM((count, depth), f32),
            pltpu.VMEM(relations.shape, f32),
            pltpu.SemaphoreType.DMA,
            pltpu.SemaphoreType.DMA,
        ],
        compiler_params=params(61),
        name="query",
    )(head_offsets, table, relations, kinds, codes)
    held = lax.all_to_all(spread.reshape(owners, stride, count), "entity", 0, 0, tiled=True)

    share_rows = owners // 2 * 16
    slots, mine, matches = pl.pallas_call(
        plan_kernel,
        out_shape=(
            jax.ShapeDtypeStruct((PARTS, 128), i32),
            jax.ShapeDtypeStruct((16, 128), f32),
            jax.ShapeDtypeStruct((2, share_rows, 32), f32),
        ),
        in_specs=[smem] + [vmem] * 2,
        scratch_shapes=[pltpu.VMEM((owners, owners), f32)],
        compiler_params=params(8),
        name="plan",
    )(me, lists, list_lengths)

    held, rounded = lax.optimization_barrier((held, table.astype(bf16)))

    def pack(*refs):
        pack_kernel(*refs, block_rows)

    packed, targets = pl.pallas_call(
        pack,
        out_shape=(
            jax.ShapeDtypeStruct((depth, CAP * count), bf16),
            jax.ShapeDtypeStruct((16, count), i32),
        ),
        in_specs=[smem, smem] + [vmem] * 2,
        scratch_shapes=[pltpu.VMEM((16, count), f32)],
        compiler_params=params(8),
        name="pack",
    )(me, slots, held.reshape(owners * stride, count), mine)
    planes = [[z * PARTS + p for p in range(PARTS)] for z in range(owners // PARTS)]
    query_t = lax.all_to_all(
        packed.reshape(PARTS, depth // PARTS, CAP * count),
        "entity",
        0,
        0,
        tiled=True,
        axis_index_groups=planes,
    ).reshape(depth, CAP * count)
    assert groups == 4
    far_t, next_t, last_t = (
        lax.ppermute(query_t, "dp", [(i, (i - shift) % groups) for i in range(groups)]) for shift in (2, 1, 3)
    )

    local = pl.pallas_call(
        stats_kernel,
        out_shape=jax.ShapeDtypeStruct((32, count), f32),
        in_specs=[vmem] * 3,
        scratch_shapes=[pltpu.VMEM((8, CAP * count), f32)] * 3,
        compiler_params=params(16),
        name="stats",
    )(query_t, rounded, targets)

    other = lax.ppermute(local, "entity", [(i, i ^ 1) for i in range(owners)])
    share = pl.pallas_call(
        share_kernel,
        out_shape=jax.ShapeDtypeStruct((share_rows, count), f32),
        in_specs=[vmem] * 3,
        compiler_params=params(8),
        name="share",
    )(matches, local, other)
    cores = [[i for i in range(owners) if i % 2 == core] for core in range(2)]
    shared = lax.all_to_all(
        share.reshape(owners // 2, 16, count), "entity", 0, 0, tiled=True, axis_index_groups=cores
    )

    info, loss = pl.pallas_call(
        merge_kernel,
        out_shape=(jax.ShapeDtypeStruct((32, count), f32), jax.ShapeDtypeStruct((1, count), f32)),
        compiler_params=params(8),
        name="merge",
    )(shared, targets)

    quarter = block_rows // groups
    half = quarter // 2
    mine_first = group.reshape(1)
    infos = lax.all_to_all(
        jnp.broadcast_to(info[None], (groups,) + info.shape), "dp", 0, 0, tiled=True
    )

    def cost(several):
        return pl.CostEstimate(
            flops=several * 4 * quarter * CAP * count * depth,
            transcendentals=several * quarter * CAP * count,
            bytes_accessed=8 * quarter * depth + several * 2 * CAP * count * depth,
        )

    own = pl.pallas_call(
        own_kernel,
        out_shape=jax.ShapeDtypeStruct((quarter, depth), f32),
        in_specs=[smem] + [vmem] * 3,
        scratch_shapes=[pltpu.VMEM((half, CAP * count), bf16)],
        compiler_params=params(16),
        cost_estimate=cost(1),
        name="own",
    )(mine_first, info, rounded, query_t)
    gradient = pl.pallas_call(
        rest_kernel,
        out_shape=jax.ShapeDtypeStruct((quarter, depth), f32),
        in_specs=[smem] + [vmem] * 2 + [pl.BlockSpec(memory_space=pltpu.HBM)] * 4,
        out_specs=pl.BlockSpec(memory_space=pltpu.HBM),
        scratch_shapes=[
            pltpu.VMEM((quarter, depth), f32),
            pltpu.VMEM((groups - 1, depth, CAP * count), bf16),
            pltpu.VMEM((half, CAP * count), bf16),
            pltpu.SemaphoreType.DMA((groups - 1,)),
            pltpu.SemaphoreType.DMA,
            pltpu.SemaphoreType.DMA((2,)),
        ],
        input_output_aliases={3: 0},
        compiler_params=params(16),
        cost_estimate=cost(groups - 1),
        name="rest",
    )(mine_first, infos, rounded, own, next_t, last_t, far_t)
    return (loss.reshape(count), gradient[None])


def solution(mesh):
    return jax.shard_map(
        per_device,
        mesh=mesh,
        in_specs=(
            P("entity", None, None),
            P("entity", None, None),
            P("dp", None),
            P("dp", None),
            P(("dp", "entity")),
            P(("dp", "entity")),
            P(("dp", "entity")),
        ),
        out_specs=(P(("dp", "entity")), P("entity", "dp", None)),
        check_vma=False,
    )
```

```python
import jax
import jax.numpy as jnp
from jax import lax
from jax.experimental import pallas as pl
from jax.experimental.pallas import tpu as pltpu
from jax.sharding import PartitionSpec as P

f32, bf16, i32 = jnp.float32, jnp.bfloat16, jnp.int32
CAP = 12
PARTS = 16
OWN_FACTOR = 6
WIDE = 4
TILE = 1024
CHUNK = 128
NEG = -1e30
NONE_ROW = 14
HIGH = lax.Precision.HIGHEST


def iota(shape, axis):
    return lax.broadcasted_iota(i32, shape, axis)


def dot(a, b, ca=1, cb=0, precision=None):
    return lax.dot_general(
        a, b, (((ca,), (cb,)), ((), ())), precision=precision, preferred_element_type=f32
    )


def whole(shape):
    return pl.BlockSpec(shape, lambda *_: (0,) * len(shape))


def query_kernel(heads, table, operators, kinds, codes, out, rows, relations, sem, other_sem):
    count = rows.shape[0]
    load = pltpu.make_async_copy(operators, relations, other_sem)
    load.start()

    def fetch(n, carry):
        pltpu.make_async_copy(
            table.at[pl.ds(heads[n], 1), :], rows.at[pl.ds(n, 1), :], sem
        ).start()
        return carry

    lax.fori_loop(0, count, fetch, 0, unroll=8)
    diagonal = iota((count, count), 0) == iota((count, count), 1)
    kind = jnp.sum(jnp.where(diagonal, kinds[...].astype(f32), 0.0), axis=1, keepdims=True)
    depth = relations.shape[2]
    part = depth // PARTS
    total = PARTS * (part + 8)
    row, column = iota((total, depth), 0), iota((total, depth), 1)
    place = row % (part + 8)
    pick = (place < part) & (row // (part + 8) * part + place == column)
    pick = pick.astype(f32).astype(bf16)
    load.wait()
    pltpu.make_async_copy(table.at[pl.ds(0, count), :], rows, sem).wait()
    head = rows[...]
    query = jnp.zeros((count, depth), f32)
    for r in range(relations.shape[0]):
        product = dot(head, relations[r], precision=HIGH)
        query = jnp.where(kind == r, product, query)
    spread = dot(pick, query.astype(bf16), 1, 1)
    place = iota(spread.shape, 0) % (part + 8)
    code = codes[...]
    spread = jnp.where(place == part, (code // 128).astype(f32), spread)
    spread = jnp.where(place == part + 1, (code % 128).astype(f32), spread)
    spread = spread.astype(bf16)
    for z in range(out.shape[0] // total):
        out[z * total : (z + 1) * total, :] = spread


def plan_kernel(me, lists, lengths, slots, mine, matches, ranks):
    sets = lists.shape[1]
    lists_t = lists[...].astype(f32)
    used_t = jnp.where(iota(lists_t.shape, 0) < lengths[...], lists_t, -1.0)
    block = iota((sets, sets), 0).astype(f32)
    listed = jnp.zeros((sets, sets), f32)
    for k in range(lists_t.shape[0]):
        listed = jnp.where(used_t[k : k + 1, :] == block, 1.0, listed)
    before = (iota((sets, sets), 0) < iota((sets, sets), 1)).astype(f32).astype(bf16)
    rank = jnp.where(listed > 0.0, dot(listed.astype(bf16), before), -1.0)
    ranks[...] = rank
    group = ranks[pl.ds(pl.multiple_of(me[0] // PARTS * PARTS, PARTS), PARTS), :]
    number = iota(group.shape, 1).astype(f32)
    lane = iota(slots.shape, 1)
    table = jnp.zeros(slots.shape, f32)
    for i in range(CAP):
        held = jnp.sum(jnp.where(group == float(i), number, 0.0), axis=1, keepdims=True)
        table = jnp.where(lane == i, held, table)
    slots[...] = table.astype(i32)
    own = ranks[pl.ds(me[0], 1), :]
    count = mine.shape[0]
    taken = own == iota((count, sets), 0).astype(f32)
    onehot = taken.astype(f32).astype(bf16)
    width = lists_t.shape[0]
    spread = (iota((width, 128), 0) == iota((width, 128), 1)).astype(f32).astype(bf16)
    padded = dot(lists_t.astype(bf16), spread, 0, 0)
    result = dot(onehot, padded.astype(bf16))
    length = jnp.sum(jnp.where(taken, lengths[...].astype(f32), 0.0), axis=1, keepdims=True)
    used = jnp.sum(taken.astype(f32), axis=1, keepdims=True)
    lane = iota(result.shape, 1)
    result = jnp.where(lane == width, length, result)
    mine[...] = jnp.where(lane == width + 1, used, result)
    total = matches.shape[1]
    core = me[0] % 2
    row = iota((total, sets), 0)
    up = (row // 16 * 2 + core == iota((total, sets), 1)).astype(f32)
    wide = dot(up.astype(bf16), rank.astype(bf16))
    slot = row % 16
    shared = (wide == slot.astype(f32)) & (slot < CAP)
    shared = shared | (((slot == CAP) | (slot == CAP + 1)) & (up > 0.5))
    shared = shared.astype(f32).astype(bf16)
    slot, source = iota((total, 32), 0) % 16, iota((total, 32), 1)
    keep = (slot == CAP + 1) == (source >= 16)
    for which, owner in enumerate((me[0], me[0] + 1 - 2 * core)):
        owned = ranks[pl.ds(owner, 1), :] == (iota((32, sets), 0) % 16).astype(f32)
        match = jnp.where(keep, dot(shared, owned.astype(f32).astype(bf16), 1, 1), 0.0)
        found = jnp.sum(match, axis=1, keepdims=True) > 0.5
        nothing = (source == NONE_ROW) & (slot != CAP + 1) & jnp.logical_not(found)
        matches[which] = jnp.where(nothing, 1.0, match)


def pack_kernel(me, slots, held, mine, out, targets, codes, block_rows):
    part = out.shape[0] // PARTS
    stride = part + 8
    for p in range(PARTS):
        for i in range(CAP):
            start = pl.multiple_of(slots[p, i] * stride, 8)
            out[p * part : (p + 1) * part, i * 128 : (i + 1) * 128] = held[pl.ds(start, part), :]
    codes[...] = jnp.zeros(codes.shape, f32)
    for i in range(CAP):
        start = pl.multiple_of(slots[me[0] % PARTS, i] * stride + part, 8)
        pair = held[pl.ds(start, 8), :].astype(f32)
        codes[i : i + 1, :] = pair[0:1, :] * 128.0 + pair[1:2, :]
    code = codes[...].astype(i32)
    info = mine[...].astype(i32)
    width = 8
    length = info[:, width : width + 1]
    used = info[:, width + 1 : width + 2] > 0
    entry = code // block_rows
    for _ in range(3):
        entry = jnp.where(entry >= length, entry - length, entry)
    block = jnp.full(code.shape, -1, i32)
    for k in range(width):
        block = jnp.where(entry == k, info[:, k : k + 1], block)
    targets[...] = jnp.where((block == me[0]) & used, code % block_rows, -1)


def stats_kernel(query_t, table, targets, out, top_s, sum_s, tgt_s):
    top_s[...] = jnp.full(top_s.shape, NEG, f32)
    sum_s[...] = jnp.zeros(sum_s.shape, f32)
    tgt_s[...] = jnp.zeros(tgt_s.shape, f32)

    def visit(step, carry):
        rows = table[pl.ds(step * TILE, TILE), :]
        for p in range(CAP // WIDE):
            columns = slice(p * WIDE * 128, (p + 1) * WIDE * 128)
            weights = query_t[:, columns]
            target = slot_lanes(targets, p)
            wanted = target - iota((8, target.shape[1]), 0) - step * TILE
            top, mass, hit = top_s[:, columns], sum_s[:, columns], tgt_s[:, columns]
            for c in range(TILE // CHUNK):
                score = dot(rows[c * CHUNK : (c + 1) * CHUNK, :], weights)
                score = score.reshape(CHUNK // 8, 8, score.shape[1])
                above = jnp.maximum(top, jnp.max(score, axis=0))
                mass = mass * jnp.exp(top - above) + jnp.sum(jnp.exp(score - above[None]), axis=0)
                top = above
                for k in range(CHUNK // 8):
                    hit = jnp.where(wanted == c * CHUNK + k * 8, score[k], hit)
            top_s[:, columns], sum_s[:, columns], tgt_s[:, columns] = top, mass, hit
        return carry

    lax.fori_loop(0, table.shape[0] // TILE, visit, 0)
    top = top_s[...]
    best = jnp.max(top, axis=0, keepdims=True)
    mass = jnp.sum(sum_s[...] * jnp.exp(top - best), axis=0, keepdims=True)
    local = best + jnp.log(mass)
    picked = jnp.sum(tgt_s[...], axis=0, keepdims=True)
    out[...] = jnp.where(iota(out.shape, 0) == NONE_ROW, NEG, 0.0)
    for i in range(CAP):
        out[i : i + 1, :] = local[:, i * 128 : (i + 1) * 128]
        out[16 + i : 17 + i, :] = picked[:, i * 128 : (i + 1) * 128]


def slot_lanes(ref, p, base=0):
    first = base + WIDE * p
    return jnp.concatenate([ref[i : i + 1, :] for i in range(first, first + WIDE)], axis=1)


def share_kernel(matches, mine, other, out):
    wants_target = iota(out.shape, 0) % 16 == CAP + 1
    first = dot(matches[0], mine[...], precision=HIGH)
    second = dot(matches[1], other[...], precision=HIGH)
    best = jnp.maximum(first, second)
    both = best + jnp.log(jnp.exp(first - best) + jnp.exp(second - best))
    out[...] = jnp.where(wants_target, first + second, both)


def merge_kernel(received, targets, info, loss):
    values = received[...]
    best = jnp.max(values, axis=0)
    mass = jnp.sum(jnp.exp(values - best[None]), axis=0)
    norm = best + jnp.log(mass)
    for group in range(info.shape[0]):
        info[group, 0:16, :] = jnp.where(best <= 0.5 * NEG, -NEG, norm)
        info[group, 16:32, :] = targets[...].astype(f32)
    target = jnp.sum(values[:, CAP + 1, :], axis=0, keepdims=True)
    loss[...] = norm[CAP : CAP + 1, :] - target


def rows_gradient(start, rows, info, query_t, coefficients, arrived=None):
    count = rows.shape[0]
    for p in range(CAP // WIDE):
        if arrived is not None:
            arrived(p)
        columns = slice(p * WIDE * 128, (p + 1) * WIDE * 128)
        weights = query_t[:, columns]
        norm = slot_lanes(info, p)
        target = slot_lanes(info, p, 16).astype(i32)
        wanted = target - iota((8, target.shape[1]), 0) - start
        for c in range(count // CHUNK):
            score = dot(rows[c * CHUNK : (c + 1) * CHUNK, :], weights)
            score = score.reshape(CHUNK // 8, 8, score.shape[1])
            weight = jnp.exp(score - norm[None])
            place = iota(score.shape, 0) * 8 + c * CHUNK
            weight = jnp.where(place == wanted[None], weight - 1.0, weight)
            coefficients[c * CHUNK : (c + 1) * CHUNK, columns] = weight.reshape(CHUNK, -1).astype(bf16)
    return dot(coefficients[...], query_t[...], 1, 1)


def own_kernel(group, info, table, query_t, out, coefficients):
    half = coefficients.shape[0]
    for h in range(out.shape[0] // half):
        start = pl.multiple_of(group[0] * out.shape[0] + h * half, half)
        rows = table[pl.ds(start, half), :]
        out[h * half : (h + 1) * half, :] = rows_gradient(start, rows, info.at[0], query_t, coefficients)


def rest_kernel(
    group, infos, table, own, next_t, last_t, far_t, out, total, queries, coefficients, load_sems, own_sem, sems
):
    half = coefficients.shape[0]
    groups = infos.shape[0]
    third = queries.shape[2] // 3
    loads = [
        [
            pltpu.make_async_copy(
                query_t.at[:, pl.ds(k * third, third)], queries.at[i, :, pl.ds(k * third, third)], load_sems.at[i, k]
            )
            for k in range(3)
        ]
        for i, query_t in enumerate((next_t, last_t, far_t))
    ]
    own_load = pltpu.make_async_copy(own, total, own_sem)
    for load in loads[0]:
        load.start()
    copies = []
    for h in range(out.shape[0] // half):
        start = pl.multiple_of(group[0] * out.shape[0] + h * half, half)
        rows = table[pl.ds(start, half), :]
        here = slice(h * half, (h + 1) * half)
        gradient = jnp.zeros((half, out.shape[1]), f32)
        for i, shift in enumerate((1, 3, 2)):

            def arrived(p, h=h, i=i):
                if h == 0:
                    loads[i][p].wait()
                    if i < 2:
                        loads[i + 1][p].start()
                    elif p == 0:
                        own_load.start()

            info = infos.at[(group[0] + shift) % groups]
            gradient = gradient + rows_gradient(start, rows, info, queries.at[i], coefficients, arrived)
        if h == 0:
            own_load.wait()
        total[here, :] = total[here, :] + gradient
        copies.append(pltpu.make_async_copy(total.at[here, :], out.at[here, :], sems.at[h]))
        copies[-1].start()
    for copy in copies:
        copy.wait()


def per_device(
    entities,
    relations,
    candidate_blocks,
    list_lengths,
    head_offsets,
    relation_offsets,
    target_codes,
):
    owners = lax.axis_size("entity")
    groups = lax.axis_size("dp")
    table = entities[0]
    block_rows, depth = table.shape
    count = head_offsets.shape[0]
    me = lax.axis_index("entity").astype(i32).reshape(1)
    group = lax.axis_index("dp").astype(i32)
    smem = pl.BlockSpec(memory_space=pltpu.SMEM)

    def params(mebibytes):
        return pltpu.CompilerParams(vmem_limit_bytes=mebibytes * 1024 * 1024)

    lists = candidate_blocks.T
    kinds = relation_offsets.reshape(1, count)
    codes = target_codes.reshape(1, count)

    vmem = pl.BlockSpec(memory_space=pltpu.VMEM)
    stride = depth // PARTS + 8
    spread = pl.pallas_call(
        query_kernel,
        out_shape=jax.ShapeDtypeStruct((owners * stride, count), bf16),
        in_specs=[smem] + [pl.BlockSpec(memory_space=pltpu.HBM)] * 2 + [vmem] * 2,
        scratch_shapes=[
            pltpu.VMEM((count, depth), f32),
            pltpu.VMEM(relations.shape, f32),
            pltpu.SemaphoreType.DMA,
            pltpu.SemaphoreType.DMA,
        ],
        compiler_params=params(61),
        name="query",
    )(head_offsets, table, relations, kinds, codes)
    held = lax.all_to_all(spread.reshape(owners, stride, count), "entity", 0, 0, tiled=True)

    share_rows = owners // 2 * 16
    slots, mine, matches = pl.pallas_call(
        plan_kernel,
        out_shape=(
            jax.ShapeDtypeStruct((PARTS, 128), i32),
            jax.ShapeDtypeStruct((16, 128), f32),
            jax.ShapeDtypeStruct((2, share_rows, 32), f32),
        ),
        in_specs=[smem] + [vmem] * 2,
        scratch_shapes=[pltpu.VMEM((owners, owners), f32)],
        compiler_params=params(8),
        name="plan",
    )(me, lists, list_lengths)

    held, rounded = lax.optimization_barrier((held, table.astype(bf16)))

    def pack(*refs):
        pack_kernel(*refs, block_rows)

    packed, targets = pl.pallas_call(
        pack,
        out_shape=(
            jax.ShapeDtypeStruct((depth, CAP * count), bf16),
            jax.ShapeDtypeStruct((16, count), i32),
        ),
        in_specs=[smem, smem] + [vmem] * 2,
        scratch_shapes=[pltpu.VMEM((16, count), f32)],
        compiler_params=params(8),
        name="pack",
    )(me, slots, held.reshape(owners * stride, count), mine)
    planes = [[z * PARTS + p for p in range(PARTS)] for z in range(owners // PARTS)]
    query_t = lax.all_to_all(
        packed.reshape(PARTS, depth // PARTS, CAP * count),
        "entity",
        0,
        0,
        tiled=True,
        axis_index_groups=planes,
    ).reshape(depth, CAP * count)

    local = pl.pallas_call(
        stats_kernel,
        out_shape=jax.ShapeDtypeStruct((32, count), f32),
        in_specs=[vmem] * 3,
        scratch_shapes=[pltpu.VMEM((8, CAP * count), f32)] * 3,
        compiler_params=params(16),
        name="stats",
    )(query_t, rounded, targets)

    other = lax.ppermute(local, "entity", [(i, i ^ 1) for i in range(owners)])
    share = pl.pallas_call(
        share_kernel,
        out_shape=jax.ShapeDtypeStruct((share_rows, count), f32),
        in_specs=[vmem] * 3,
        compiler_params=params(8),
        name="share",
    )(matches, local, other)
    assert groups == 4
    share, sent_t = lax.optimization_barrier((share, query_t))
    far_t, next_t, last_t = (
        lax.ppermute(sent_t, "dp", [(i, (i - shift) % groups) for i in range(groups)]) for shift in (2, 1, 3)
    )
    cores = [[i for i in range(owners) if i % 2 == core] for core in range(2)]
    shared = lax.all_to_all(
        share.reshape(owners // 2, 16, count), "entity", 0, 0, tiled=True, axis_index_groups=cores
    )

    info, loss = pl.pallas_call(
        merge_kernel,
        out_shape=(jax.ShapeDtypeStruct((groups, 32, count), f32), jax.ShapeDtypeStruct((1, count), f32)),
        compiler_params=params(8),
        name="merge",
    )(shared, targets)

    quarter = block_rows // groups
    half = quarter // 2
    mine_first = group.reshape(1)
    infos = lax.all_to_all(info, "dp", 0, 0, tiled=True)

    def cost(several, factor=1):
        several = several * factor
        return pl.CostEstimate(
            flops=several * 4 * quarter * CAP * count * depth,
            transcendentals=several * quarter * CAP * count,
            bytes_accessed=8 * quarter * depth + several * 2 * CAP * count * depth,
        )

    own = pl.pallas_call(
        own_kernel,
        out_shape=jax.ShapeDtypeStruct((quarter, depth), f32),
        in_specs=[smem] + [vmem] * 3,
        scratch_shapes=[pltpu.VMEM((half, CAP * count), bf16)],
        compiler_params=params(16),
        cost_estimate=cost(1, OWN_FACTOR),
        name="own",
    )(mine_first, info, rounded, query_t)
    gradient = pl.pallas_call(
        rest_kernel,
        out_shape=jax.ShapeDtypeStruct((quarter, depth), f32),
        in_specs=[smem] + [vmem] * 2 + [pl.BlockSpec(memory_space=pltpu.HBM)] * 4,
        out_specs=pl.BlockSpec(memory_space=pltpu.HBM),
        scratch_shapes=[
            pltpu.VMEM((quarter, depth), f32),
            pltpu.VMEM((groups - 1, depth, CAP * count), bf16),
            pltpu.VMEM((half, CAP * count), bf16),
            pltpu.SemaphoreType.DMA((groups - 1, 3)),
            pltpu.SemaphoreType.DMA,
            pltpu.SemaphoreType.DMA((2,)),
        ],
        input_output_aliases={3: 0},
        compiler_params=params(16),
        cost_estimate=cost(groups - 1),
        name="rest",
    )(mine_first, infos, rounded, own, next_t, last_t, far_t)
    return (loss.reshape(count), gradient[None])


def solution(mesh):
    return jax.shard_map(
        per_device,
        mesh=mesh,
        in_specs=(
            P("entity", None, None),
            P("entity", None, None),
            P("dp", None),
            P("dp", None),
            P(("dp", "entity")),
            P(("dp", "entity")),
            P(("dp", "entity")),
        ),
        out_specs=(P(("dp", "entity")), P("entity", "dp", None)),
        check_vma=False,
    )
```

```python
import jax
import jax.numpy as jnp
from jax import lax
from jax.experimental import pallas as pl
from jax.experimental.pallas import tpu as pltpu
from jax.sharding import PartitionSpec as P

f32, bf16, i32 = jnp.float32, jnp.bfloat16, jnp.int32
CAP = 12
PARTS = 16
WIDE = 4
TILE = 1024
CHUNK = 128
NEG = -1e30
NONE_ROW = 14
HIGH = lax.Precision.HIGHEST


def iota(shape, axis):
    return lax.broadcasted_iota(i32, shape, axis)


def dot(a, b, ca=1, cb=0, precision=None):
    return lax.dot_general(
        a, b, (((ca,), (cb,)), ((), ())), precision=precision, preferred_element_type=f32
    )


def whole(shape):
    return pl.BlockSpec(shape, lambda *_: (0,) * len(shape))


def query_kernel(heads, table, operators, kinds, codes, out, rows, relations, sem, other_sem):
    count = rows.shape[0]
    load = pltpu.make_async_copy(operators, relations, other_sem)
    load.start()

    def fetch(n, carry):
        pltpu.make_async_copy(
            table.at[pl.ds(heads[n], 1), :], rows.at[pl.ds(n, 1), :], sem
        ).start()
        return carry

    lax.fori_loop(0, count, fetch, 0, unroll=8)
    diagonal = iota((count, count), 0) == iota((count, count), 1)
    kind = jnp.sum(jnp.where(diagonal, kinds[...].astype(f32), 0.0), axis=1, keepdims=True)
    depth = relations.shape[2]
    part = depth // PARTS
    total = PARTS * (part + 8)
    row, column = iota((total, depth), 0), iota((total, depth), 1)
    place = row % (part + 8)
    pick = (place < part) & (row // (part + 8) * part + place == column)
    pick = pick.astype(f32).astype(bf16)
    load.wait()
    pltpu.make_async_copy(table.at[pl.ds(0, count), :], rows, sem).wait()
    head = rows[...]
    query = jnp.zeros((count, depth), f32)
    for r in range(relations.shape[0]):
        product = dot(head, relations[r], precision=HIGH)
        query = jnp.where(kind == r, product, query)
    spread = dot(pick, query.astype(bf16), 1, 1)
    place = iota(spread.shape, 0) % (part + 8)
    code = codes[...]
    spread = jnp.where(place == part, (code // 128).astype(f32), spread)
    spread = jnp.where(place == part + 1, (code % 128).astype(f32), spread)
    spread = spread.astype(bf16)
    for z in range(out.shape[0] // total):
        out[z * total : (z + 1) * total, :] = spread


def plan_kernel(me, lists, lengths, slots, mine, matches, ranks):
    sets = lists.shape[1]
    lists_t = lists[...].astype(f32)
    used_t = jnp.where(iota(lists_t.shape, 0) < lengths[...], lists_t, -1.0)
    block = iota((sets, sets), 0).astype(f32)
    listed = jnp.zeros((sets, sets), f32)
    for k in range(lists_t.shape[0]):
        listed = jnp.where(used_t[k : k + 1, :] == block, 1.0, listed)
    before = (iota((sets, sets), 0) < iota((sets, sets), 1)).astype(f32).astype(bf16)
    rank = jnp.where(listed > 0.0, dot(listed.astype(bf16), before), -1.0)
    ranks[...] = rank
    group = ranks[pl.ds(pl.multiple_of(me[0] // PARTS * PARTS, PARTS), PARTS), :]
    number = iota(group.shape, 1).astype(f32)
    lane = iota(slots.shape, 1)
    table = jnp.zeros(slots.shape, f32)
    for i in range(CAP):
        held = jnp.sum(jnp.where(group == float(i), number, 0.0), axis=1, keepdims=True)
        table = jnp.where(lane == i, held, table)
    slots[...] = table.astype(i32)
    own = ranks[pl.ds(me[0], 1), :]
    count = mine.shape[0]
    taken = own == iota((count, sets), 0).astype(f32)
    onehot = taken.astype(f32).astype(bf16)
    width = lists_t.shape[0]
    spread = (iota((width, 128), 0) == iota((width, 128), 1)).astype(f32).astype(bf16)
    padded = dot(lists_t.astype(bf16), spread, 0, 0)
    result = dot(onehot, padded.astype(bf16))
    length = jnp.sum(jnp.where(taken, lengths[...].astype(f32), 0.0), axis=1, keepdims=True)
    used = jnp.sum(taken.astype(f32), axis=1, keepdims=True)
    lane = iota(result.shape, 1)
    result = jnp.where(lane == width, length, result)
    mine[...] = jnp.where(lane == width + 1, used, result)
    total = matches.shape[1]
    core = me[0] % 2
    row = iota((total, sets), 0)
    up = (row // 16 * 2 + core == iota((total, sets), 1)).astype(f32)
    wide = dot(up.astype(bf16), rank.astype(bf16))
    slot = row % 16
    shared = (wide == slot.astype(f32)) & (slot < CAP)
    shared = shared | (((slot == CAP) | (slot == CAP + 1)) & (up > 0.5))
    shared = shared.astype(f32).astype(bf16)
    slot, source = iota((total, 32), 0) % 16, iota((total, 32), 1)
    keep = (slot == CAP + 1) == (source >= 16)
    for which, owner in enumerate((me[0], me[0] + 1 - 2 * core)):
        owned = ranks[pl.ds(owner, 1), :] == (iota((32, sets), 0) % 16).astype(f32)
        match = jnp.where(keep, dot(shared, owned.astype(f32).astype(bf16), 1, 1), 0.0)
        found = jnp.sum(match, axis=1, keepdims=True) > 0.5
        nothing = (source == NONE_ROW) & (slot != CAP + 1) & jnp.logical_not(found)
        matches[which] = jnp.where(nothing, 1.0, match)


def pack_kernel(me, slots, held, mine, out, targets, codes, block_rows):
    part = out.shape[0] // PARTS
    stride = part + 8
    for p in range(PARTS):
        for i in range(CAP):
            start = pl.multiple_of(slots[p, i] * stride, 8)
            out[p * part : (p + 1) * part, i * 128 : (i + 1) * 128] = held[pl.ds(start, part), :]
    codes[...] = jnp.zeros(codes.shape, f32)
    for i in range(CAP):
        start = pl.multiple_of(slots[me[0] % PARTS, i] * stride + part, 8)
        pair = held[pl.ds(start, 8), :].astype(f32)
        codes[i : i + 1, :] = pair[0:1, :] * 128.0 + pair[1:2, :]
    code = codes[...].astype(i32)
    info = mine[...].astype(i32)
    width = 8
    length = info[:, width : width + 1]
    used = info[:, width + 1 : width + 2] > 0
    entry = code // block_rows
    for _ in range(3):
        entry = jnp.where(entry >= length, entry - length, entry)
    block = jnp.full(code.shape, -1, i32)
    for k in range(width):
        block = jnp.where(entry == k, info[:, k : k + 1], block)
    targets[...] = jnp.where((block == me[0]) & used, code % block_rows, -1)


def stats_kernel(query_t, table, targets, out, top_s, sum_s, tgt_s):
    top_s[...] = jnp.full(top_s.shape, NEG, f32)
    sum_s[...] = jnp.zeros(sum_s.shape, f32)
    tgt_s[...] = jnp.zeros(tgt_s.shape, f32)

    def visit(step, carry):
        rows = table[pl.ds(step * TILE, TILE), :]
        for p in range(CAP // WIDE):
            columns = slice(p * WIDE * 128, (p + 1) * WIDE * 128)
            weights = query_t[:, columns]
            target = slot_lanes(targets, p)
            wanted = target - iota((8, target.shape[1]), 0) - step * TILE
            top, mass, hit = top_s[:, columns], sum_s[:, columns], tgt_s[:, columns]
            for c in range(TILE // CHUNK):
                score = dot(rows[c * CHUNK : (c + 1) * CHUNK, :], weights)
                score = score.reshape(CHUNK // 8, 8, score.shape[1])
                above = jnp.maximum(top, jnp.max(score, axis=0))
                mass = mass * jnp.exp(top - above) + jnp.sum(jnp.exp(score - above[None]), axis=0)
                top = above
                for k in range(CHUNK // 8):
                    hit = jnp.where(wanted == c * CHUNK + k * 8, score[k], hit)
            top_s[:, columns], sum_s[:, columns], tgt_s[:, columns] = top, mass, hit
        return carry

    lax.fori_loop(0, table.shape[0] // TILE, visit, 0)
    top = top_s[...]
    best = jnp.max(top, axis=0, keepdims=True)
    mass = jnp.sum(sum_s[...] * jnp.exp(top - best), axis=0, keepdims=True)
    local = best + jnp.log(mass)
    picked = jnp.sum(tgt_s[...], axis=0, keepdims=True)
    out[...] = jnp.where(iota(out.shape, 0) == NONE_ROW, NEG, 0.0)
    for i in range(CAP):
        out[i : i + 1, :] = local[:, i * 128 : (i + 1) * 128]
        out[16 + i : 17 + i, :] = picked[:, i * 128 : (i + 1) * 128]


def slot_lanes(ref, p, base=0):
    first = base + WIDE * p
    return jnp.concatenate([ref[i : i + 1, :] for i in range(first, first + WIDE)], axis=1)


def share_kernel(matches, mine, other, out):
    wants_target = iota(out.shape, 0) % 16 == CAP + 1
    first = dot(matches[0], mine[...], precision=HIGH)
    second = dot(matches[1], other[...], precision=HIGH)
    best = jnp.maximum(first, second)
    both = best + jnp.log(jnp.exp(first - best) + jnp.exp(second - best))
    out[...] = jnp.where(wants_target, first + second, both)


def merge_kernel(received, targets, info, loss):
    values = received[...]
    best = jnp.max(values, axis=0)
    mass = jnp.sum(jnp.exp(values - best[None]), axis=0)
    norm = best + jnp.log(mass)
    for group in range(info.shape[0]):
        info[group, 0:16, :] = jnp.where(best <= 0.5 * NEG, -NEG, norm)
        info[group, 16:32, :] = targets[...].astype(f32)
    target = jnp.sum(values[:, CAP + 1, :], axis=0, keepdims=True)
    loss[...] = norm[CAP : CAP + 1, :] - target


def rows_gradient(start, rows, info, query_t, coefficients):
    count = rows.shape[0]
    for p in range(CAP // WIDE):
        columns = slice(p * WIDE * 128, (p + 1) * WIDE * 128)
        weights = query_t[:, columns]
        norm = slot_lanes(info, p)
        target = slot_lanes(info, p, 16).astype(i32)
        wanted = target - iota((8, target.shape[1]), 0) - start
        for c in range(count // CHUNK):
            score = dot(rows[c * CHUNK : (c + 1) * CHUNK, :], weights)
            score = score.reshape(CHUNK // 8, 8, score.shape[1])
            weight = jnp.exp(score - norm[None])
            place = iota(score.shape, 0) * 8 + c * CHUNK
            weight = jnp.where(place == wanted[None], weight - 1.0, weight)
            coefficients[c * CHUNK : (c + 1) * CHUNK, columns] = weight.reshape(CHUNK, -1).astype(bf16)
    return dot(coefficients[...], query_t[...], 1, 1)


def own_kernel(group, info, table, query_t, out, coefficients):
    half = coefficients.shape[0]
    for h in range(out.shape[0] // half):
        start = pl.multiple_of(group[0] * out.shape[0] + h * half, half)
        rows = table[pl.ds(start, half), :]
        out[h * half : (h + 1) * half, :] = rows_gradient(start, rows, info.at[0], query_t, coefficients)


def rest_kernel(
    group, infos, table, own, next_t, last_t, far_low, far_high, out, total, queries, coefficients, load_sems, own_sem, sems
):
    half = coefficients.shape[0]
    groups = infos.shape[0]
    low = far_low.shape[0]
    loads = [
        [pltpu.make_async_copy(next_t, queries.at[0], load_sems.at[0])],
        [pltpu.make_async_copy(last_t, queries.at[1], load_sems.at[1])],
        [
            pltpu.make_async_copy(far_low, queries.at[2, pl.ds(0, low), :], load_sems.at[2]),
            pltpu.make_async_copy(far_high, queries.at[2, pl.ds(low, low), :], load_sems.at[3]),
        ],
        [pltpu.make_async_copy(own, total, own_sem)],
    ]

    def start_all(i):
        for load in loads[i]:
            load.start()

    def wait_all(i):
        for load in loads[i]:
            load.wait()

    start_all(0)
    copies = []
    for h in range(out.shape[0] // half):
        start = pl.multiple_of(group[0] * out.shape[0] + h * half, half)
        rows = table[pl.ds(start, half), :]
        here = slice(h * half, (h + 1) * half)
        gradient = jnp.zeros((half, out.shape[1]), f32)
        for i, shift in enumerate((1, 3, 2)):
            if h == 0:
                wait_all(i)
                start_all(i + 1)
            info = infos.at[(group[0] + shift) % groups]
            gradient = gradient + rows_gradient(start, rows, info, queries.at[i], coefficients)
        if h == 0:
            wait_all(groups - 1)
        total[here, :] = total[here, :] + gradient
        copies.append(pltpu.make_async_copy(total.at[here, :], out.at[here, :], sems.at[h]))
        copies[-1].start()
    for copy in copies:
        copy.wait()


def per_device(
    entities,
    relations,
    candidate_blocks,
    list_lengths,
    head_offsets,
    relation_offsets,
    target_codes,
):
    owners = lax.axis_size("entity")
    groups = lax.axis_size("dp")
    table = entities[0]
    block_rows, depth = table.shape
    count = head_offsets.shape[0]
    me = lax.axis_index("entity").astype(i32).reshape(1)
    group = lax.axis_index("dp").astype(i32)
    smem = pl.BlockSpec(memory_space=pltpu.SMEM)

    def params(mebibytes):
        return pltpu.CompilerParams(vmem_limit_bytes=mebibytes * 1024 * 1024)

    lists = candidate_blocks.T
    kinds = relation_offsets.reshape(1, count)
    codes = target_codes.reshape(1, count)

    vmem = pl.BlockSpec(memory_space=pltpu.VMEM)
    stride = depth // PARTS + 8
    spread = pl.pallas_call(
        query_kernel,
        out_shape=jax.ShapeDtypeStruct((owners * stride, count), bf16),
        in_specs=[smem] + [pl.BlockSpec(memory_space=pltpu.HBM)] * 2 + [vmem] * 2,
        scratch_shapes=[
            pltpu.VMEM((count, depth), f32),
            pltpu.VMEM(relations.shape, f32),
            pltpu.SemaphoreType.DMA,
            pltpu.SemaphoreType.DMA,
        ],
        compiler_params=params(61),
        name="query",
    )(head_offsets, table, relations, kinds, codes)
    held = lax.all_to_all(spread.reshape(owners, stride, count), "entity", 0, 0, tiled=True)

    share_rows = owners // 2 * 16
    slots, mine, matches = pl.pallas_call(
        plan_kernel,
        out_shape=(
            jax.ShapeDtypeStruct((PARTS, 128), i32),
            jax.ShapeDtypeStruct((16, 128), f32),
            jax.ShapeDtypeStruct((2, share_rows, 32), f32),
        ),
        in_specs=[smem] + [vmem] * 2,
        scratch_shapes=[pltpu.VMEM((owners, owners), f32)],
        compiler_params=params(8),
        name="plan",
    )(me, lists, list_lengths)

    held, rounded = lax.optimization_barrier((held, table.astype(bf16)))

    def pack(*refs):
        pack_kernel(*refs, block_rows)

    packed, targets = pl.pallas_call(
        pack,
        out_shape=(
            jax.ShapeDtypeStruct((depth, CAP * count), bf16),
            jax.ShapeDtypeStruct((16, count), i32),
        ),
        in_specs=[smem, smem] + [vmem] * 2,
        scratch_shapes=[pltpu.VMEM((16, count), f32)],
        compiler_params=params(8),
        name="pack",
    )(me, slots, held.reshape(owners * stride, count), mine)
    planes = [[z * PARTS + p for p in range(PARTS)] for z in range(owners // PARTS)]
    query_t = lax.all_to_all(
        packed.reshape(PARTS, depth // PARTS, CAP * count),
        "entity",
        0,
        0,
        tiled=True,
        axis_index_groups=planes,
    ).reshape(depth, CAP * count)
    assert groups == 4
    up = [(i, (i + 1) % groups) for i in range(groups)]
    down = [(i, (i - 1) % groups) for i in range(groups)]
    last_t, next_t = lax.ppermute(query_t, "dp", up), lax.ppermute(query_t, "dp", down)

    local = pl.pallas_call(
        stats_kernel,
        out_shape=jax.ShapeDtypeStruct((32, count), f32),
        in_specs=[vmem] * 3,
        scratch_shapes=[pltpu.VMEM((8, CAP * count), f32)] * 3,
        compiler_params=params(16),
        name="stats",
    )(query_t, rounded, targets)

    other = lax.ppermute(local, "entity", [(i, i ^ 1) for i in range(owners)])
    share = pl.pallas_call(
        share_kernel,
        out_shape=jax.ShapeDtypeStruct((share_rows, count), f32),
        in_specs=[vmem] * 3,
        compiler_params=params(8),
        name="share",
    )(matches, local, other)
    _, relay_last, relay_next = lax.optimization_barrier((share, last_t, next_t))
    far_low = lax.ppermute(relay_last[: depth // 2], "dp", up)
    far_high = lax.ppermute(relay_next[depth // 2 :], "dp", down)
    cores = [[i for i in range(owners) if i % 2 == core] for core in range(2)]
    shared = lax.all_to_all(
        share.reshape(owners // 2, 16, count), "entity", 0, 0, tiled=True, axis_index_groups=cores
    )

    info, loss = pl.pallas_call(
        merge_kernel,
        out_shape=(jax.ShapeDtypeStruct((groups, 32, count), f32), jax.ShapeDtypeStruct((1, count), f32)),
        compiler_params=params(8),
        name="merge",
    )(shared, targets)

    quarter = block_rows // groups
    half = quarter // 2
    mine_first = group.reshape(1)
    infos = lax.all_to_all(info, "dp", 0, 0, tiled=True)

    def cost(several):
        return pl.CostEstimate(
            flops=several * 4 * quarter * CAP * count * depth,
            transcendentals=several * quarter * CAP * count,
            bytes_accessed=8 * quarter * depth + several * 2 * CAP * count * depth,
        )

    own = pl.pallas_call(
        own_kernel,
        out_shape=jax.ShapeDtypeStruct((quarter, depth), f32),
        in_specs=[smem] + [vmem] * 3,
        scratch_shapes=[pltpu.VMEM((half, CAP * count), bf16)],
        compiler_params=params(16),
        cost_estimate=cost(1),
        name="own",
    )(mine_first, info, rounded, query_t)
    gradient = pl.pallas_call(
        rest_kernel,
        out_shape=jax.ShapeDtypeStruct((quarter, depth), f32),
        in_specs=[smem] + [vmem] * 2 + [pl.BlockSpec(memory_space=pltpu.HBM)] * 5,
        out_specs=pl.BlockSpec(memory_space=pltpu.HBM),
        scratch_shapes=[
            pltpu.VMEM((quarter, depth), f32),
            pltpu.VMEM((groups - 1, depth, CAP * count), bf16),
            pltpu.VMEM((half, CAP * count), bf16),
            pltpu.SemaphoreType.DMA((groups,)),
            pltpu.SemaphoreType.DMA,
            pltpu.SemaphoreType.DMA((2,)),
        ],
        input_output_aliases={3: 0},
        compiler_params=params(16),
        cost_estimate=cost(groups - 1),
        name="rest",
    )(mine_first, infos, rounded, own, next_t, last_t, far_low, far_high)
    return (loss.reshape(count), gradient[None])


def solution(mesh):
    return jax.shard_map(
        per_device,
        mesh=mesh,
        in_specs=(
            P("entity", None, None),
            P("entity", None, None),
            P("dp", None),
            P("dp", None),
            P(("dp", "entity")),
            P(("dp", "entity")),
            P(("dp", "entity")),
        ),
        out_specs=(P(("dp", "entity")), P("entity", "dp", None)),
        check_vma=False,
    )
```

```python
import jax
import jax.numpy as jnp
from jax import lax
from jax.experimental import pallas as pl
from jax.experimental.pallas import tpu as pltpu
from jax.sharding import PartitionSpec as P

f32, bf16, i32 = jnp.float32, jnp.bfloat16, jnp.int32
CAP = 12
PARTS = 16
WIDE = 4
TILE = 2048
CHUNK = 128
NEG = -1e30
NONE_ROW = 14
HIGH = lax.Precision.HIGHEST


def iota(shape, axis):
    return lax.broadcasted_iota(i32, shape, axis)


def dot(a, b, ca=1, cb=0, precision=None):
    return lax.dot_general(
        a, b, (((ca,), (cb,)), ((), ())), precision=precision, preferred_element_type=f32
    )


def whole(shape):
    return pl.BlockSpec(shape, lambda *_: (0,) * len(shape))


def query_kernel(heads, table, operators, kinds, codes, out, rows, relations, sem, other_sem):
    count = rows.shape[0]
    load = pltpu.make_async_copy(operators, relations, other_sem)
    load.start()

    def fetch(n, carry):
        pltpu.make_async_copy(
            table.at[pl.ds(heads[n], 1), :], rows.at[pl.ds(n, 1), :], sem
        ).start()
        return carry

    lax.fori_loop(0, count, fetch, 0, unroll=8)
    diagonal = iota((count, count), 0) == iota((count, count), 1)
    kind = jnp.sum(jnp.where(diagonal, kinds[...].astype(f32), 0.0), axis=1, keepdims=True)
    depth = relations.shape[2]
    part = depth // PARTS
    total = PARTS * (part + 8)
    row, column = iota((total, depth), 0), iota((total, depth), 1)
    place = row % (part + 8)
    pick = (place < part) & (row // (part + 8) * part + place == column)
    pick = pick.astype(f32).astype(bf16)
    load.wait()
    pltpu.make_async_copy(table.at[pl.ds(0, count), :], rows, sem).wait()
    head = rows[...]
    query = jnp.zeros((count, depth), f32)
    for r in range(relations.shape[0]):
        product = dot(head, relations[r], precision=HIGH)
        query = jnp.where(kind == r, product, query)
    spread = dot(pick, query.astype(bf16), 1, 1)
    place = iota(spread.shape, 0) % (part + 8)
    code = codes[...]
    spread = jnp.where(place == part, (code // 128).astype(f32), spread)
    spread = jnp.where(place == part + 1, (code % 128).astype(f32), spread)
    spread = spread.astype(bf16)
    for z in range(out.shape[0] // total):
        out[z * total : (z + 1) * total, :] = spread


def plan_kernel(me, lists, lengths, slots, mine, matches, ranks):
    sets = lists.shape[1]
    lists_t = lists[...].astype(f32)
    used_t = jnp.where(iota(lists_t.shape, 0) < lengths[...], lists_t, -1.0)
    block = iota((sets, sets), 0).astype(f32)
    listed = jnp.zeros((sets, sets), f32)
    for k in range(lists_t.shape[0]):
        listed = jnp.where(used_t[k : k + 1, :] == block, 1.0, listed)
    before = (iota((sets, sets), 0) < iota((sets, sets), 1)).astype(f32).astype(bf16)
    rank = jnp.where(listed > 0.0, dot(listed.astype(bf16), before), -1.0)
    ranks[...] = rank
    group = ranks[pl.ds(pl.multiple_of(me[0] // PARTS * PARTS, PARTS), PARTS), :]
    number = iota(group.shape, 1).astype(f32)
    lane = iota(slots.shape, 1)
    table = jnp.zeros(slots.shape, f32)
    for i in range(CAP):
        held = jnp.sum(jnp.where(group == float(i), number, 0.0), axis=1, keepdims=True)
        table = jnp.where(lane == i, held, table)
    slots[...] = table.astype(i32)
    own = ranks[pl.ds(me[0], 1), :]
    count = mine.shape[0]
    taken = own == iota((count, sets), 0).astype(f32)
    onehot = taken.astype(f32).astype(bf16)
    width = lists_t.shape[0]
    spread = (iota((width, 128), 0) == iota((width, 128), 1)).astype(f32).astype(bf16)
    padded = dot(lists_t.astype(bf16), spread, 0, 0)
    result = dot(onehot, padded.astype(bf16))
    length = jnp.sum(jnp.where(taken, lengths[...].astype(f32), 0.0), axis=1, keepdims=True)
    used = jnp.sum(taken.astype(f32), axis=1, keepdims=True)
    lane = iota(result.shape, 1)
    result = jnp.where(lane == width, length, result)
    mine[...] = jnp.where(lane == width + 1, used, result)
    total = matches.shape[1]
    core = me[0] % 2
    row = iota((total, sets), 0)
    up = (row // 16 * 2 + core == iota((total, sets), 1)).astype(f32)
    wide = dot(up.astype(bf16), rank.astype(bf16))
    slot = row % 16
    shared = (wide == slot.astype(f32)) & (slot < CAP)
    shared = shared | (((slot == CAP) | (slot == CAP + 1)) & (up > 0.5))
    shared = shared.astype(f32).astype(bf16)
    slot, source = iota((total, 32), 0) % 16, iota((total, 32), 1)
    keep = (slot == CAP + 1) == (source >= 16)
    for which, owner in enumerate((me[0], me[0] + 1 - 2 * core)):
        owned = ranks[pl.ds(owner, 1), :] == (iota((32, sets), 0) % 16).astype(f32)
        match = jnp.where(keep, dot(shared, owned.astype(f32).astype(bf16), 1, 1), 0.0)
        found = jnp.sum(match, axis=1, keepdims=True) > 0.5
        nothing = (source == NONE_ROW) & (slot != CAP + 1) & jnp.logical_not(found)
        matches[which] = jnp.where(nothing, 1.0, match)


def pack_kernel(me, slots, held, mine, out, targets, codes, block_rows):
    part = out.shape[0] // PARTS
    stride = part + 8
    for p in range(PARTS):
        for i in range(CAP):
            start = pl.multiple_of(slots[p, i] * stride, 8)
            out[p * part : (p + 1) * part, i * 128 : (i + 1) * 128] = held[pl.ds(start, part), :]
    codes[...] = jnp.zeros(codes.shape, f32)
    for i in range(CAP):
        start = pl.multiple_of(slots[me[0] % PARTS, i] * stride + part, 8)
        pair = held[pl.ds(start, 8), :].astype(f32)
        codes[i : i + 1, :] = pair[0:1, :] * 128.0 + pair[1:2, :]
    code = codes[...].astype(i32)
    info = mine[...].astype(i32)
    width = 8
    length = info[:, width : width + 1]
    used = info[:, width + 1 : width + 2] > 0
    entry = code // block_rows
    for _ in range(3):
        entry = jnp.where(entry >= length, entry - length, entry)
    block = jnp.full(code.shape, -1, i32)
    for k in range(width):
        block = jnp.where(entry == k, info[:, k : k + 1], block)
    targets[...] = jnp.where((block == me[0]) & used, code % block_rows, -1)


def stats_kernel(query_t, table, targets, out, top_s, sum_s, tgt_s):
    top_s[...] = jnp.full(top_s.shape, NEG, f32)
    sum_s[...] = jnp.zeros(sum_s.shape, f32)
    tgt_s[...] = jnp.zeros(tgt_s.shape, f32)

    def visit(step, carry):
        rows = table[pl.ds(step * TILE, TILE), :]
        for p in range(CAP // WIDE):
            columns = slice(p * WIDE * 128, (p + 1) * WIDE * 128)
            weights = query_t[:, columns]
            target = slot_lanes(targets, p)
            wanted = target - iota((8, target.shape[1]), 0) - step * TILE
            top, mass, hit = top_s[:, columns], sum_s[:, columns], tgt_s[:, columns]
            for c in range(TILE // CHUNK):
                score = dot(rows[c * CHUNK : (c + 1) * CHUNK, :], weights)
                score = score.reshape(CHUNK // 8, 8, score.shape[1])
                above = jnp.maximum(top, jnp.max(score, axis=0))
                mass = mass * jnp.exp(top - above) + jnp.sum(jnp.exp(score - above[None]), axis=0)
                top = above
                for k in range(CHUNK // 8):
                    hit = jnp.where(wanted == c * CHUNK + k * 8, score[k], hit)
            top_s[:, columns], sum_s[:, columns], tgt_s[:, columns] = top, mass, hit
        return carry

    lax.fori_loop(0, table.shape[0] // TILE, visit, 0)
    top = top_s[...]
    best = jnp.max(top, axis=0, keepdims=True)
    mass = jnp.sum(sum_s[...] * jnp.exp(top - best), axis=0, keepdims=True)
    local = best + jnp.log(mass)
    picked = jnp.sum(tgt_s[...], axis=0, keepdims=True)
    out[...] = jnp.where(iota(out.shape, 0) == NONE_ROW, NEG, 0.0)
    for i in range(CAP):
        out[i : i + 1, :] = local[:, i * 128 : (i + 1) * 128]
        out[16 + i : 17 + i, :] = picked[:, i * 128 : (i + 1) * 128]


def slot_lanes(ref, p, base=0):
    first = base + WIDE * p
    return jnp.concatenate([ref[i : i + 1, :] for i in range(first, first + WIDE)], axis=1)


def share_kernel(matches, mine, other, out):
    wants_target = iota(out.shape, 0) % 16 == CAP + 1
    first = dot(matches[0], mine[...], precision=HIGH)
    second = dot(matches[1], other[...], precision=HIGH)
    best = jnp.maximum(first, second)
    both = best + jnp.log(jnp.exp(first - best) + jnp.exp(second - best))
    out[...] = jnp.where(wants_target, first + second, both)


def merge_kernel(received, targets, info, loss):
    values = received[...]
    best = jnp.max(values, axis=0)
    mass = jnp.sum(jnp.exp(values - best[None]), axis=0)
    norm = best + jnp.log(mass)
    for group in range(info.shape[0]):
        info[group, 0:16, :] = jnp.where(best <= 0.5 * NEG, -NEG, norm)
        info[group, 16:32, :] = targets[...].astype(f32)
    target = jnp.sum(values[:, CAP + 1, :], axis=0, keepdims=True)
    loss[...] = norm[CAP : CAP + 1, :] - target


def rows_gradient(start, rows, info, query_t, coefficients):
    count = rows.shape[0]
    for p in range(CAP // WIDE):
        columns = slice(p * WIDE * 128, (p + 1) * WIDE * 128)
        weights = query_t[:, columns]
        norm = slot_lanes(info, p)
        target = slot_lanes(info, p, 16).astype(i32)
        wanted = target - iota((8, target.shape[1]), 0) - start
        for c in range(count // CHUNK):
            score = dot(rows[c * CHUNK : (c + 1) * CHUNK, :], weights)
            score = score.reshape(CHUNK // 8, 8, score.shape[1])
            weight = jnp.exp(score - norm[None])
            place = iota(score.shape, 0) * 8 + c * CHUNK
            weight = jnp.where(place == wanted[None], weight - 1.0, weight)
            coefficients[c * CHUNK : (c + 1) * CHUNK, columns] = weight.reshape(CHUNK, -1).astype(bf16)
    return dot(coefficients[...], query_t[...], 1, 1)


def own_kernel(group, info, table, query_t, out, coefficients):
    half = coefficients.shape[0]
    for h in range(out.shape[0] // half):
        start = pl.multiple_of(group[0] * out.shape[0] + h * half, half)
        rows = table[pl.ds(start, half), :]
        out[h * half : (h + 1) * half, :] = rows_gradient(start, rows, info.at[0], query_t, coefficients)


def rest_kernel(
    group, infos, table, own, next_t, last_t, far_low, far_high, out, total, queries, coefficients, load_sems, own_sem, sems
):
    half = coefficients.shape[0]
    groups = infos.shape[0]
    low = far_low.shape[0]
    loads = [
        [pltpu.make_async_copy(next_t, queries.at[0], load_sems.at[0])],
        [pltpu.make_async_copy(last_t, queries.at[1], load_sems.at[1])],
        [
            pltpu.make_async_copy(far_low, queries.at[2, pl.ds(0, low), :], load_sems.at[2]),
            pltpu.make_async_copy(far_high, queries.at[2, pl.ds(low, low), :], load_sems.at[3]),
        ],
        [pltpu.make_async_copy(own, total, own_sem)],
    ]

    def start_all(i):
        for load in loads[i]:
            load.start()

    def wait_all(i):
        for load in loads[i]:
            load.wait()

    start_all(0)
    wait_all(0)
    start_all(groups - 1)
    start_all(1)
    copies = []
    for h in range(out.shape[0] // half):
        start = pl.multiple_of(group[0] * out.shape[0] + h * half, half)
        rows = table[pl.ds(start, half), :]
        here = slice(h * half, (h + 1) * half)
        for i, shift in enumerate((1, 3, 2)):
            if h == 0 and i > 0:
                wait_all(i)
            if h == 0 and i == 1:
                start_all(2)
            info = infos.at[(group[0] + shift) % groups]
            gradient = rows_gradient(start, rows, info, queries.at[i], coefficients)
            if h == 0 and i == 0:
                wait_all(groups - 1)
            total[here, :] = total[here, :] + gradient
        copies.append(pltpu.make_async_copy(total.at[here, :], out.at[here, :], sems.at[h]))
        copies[-1].start()
    for copy in copies:
        copy.wait()


def per_device(
    entities,
    relations,
    candidate_blocks,
    list_lengths,
    head_offsets,
    relation_offsets,
    target_codes,
):
    owners = lax.axis_size("entity")
    groups = lax.axis_size("dp")
    table = entities[0]
    block_rows, depth = table.shape
    count = head_offsets.shape[0]
    me = lax.axis_index("entity").astype(i32).reshape(1)
    group = lax.axis_index("dp").astype(i32)
    smem = pl.BlockSpec(memory_space=pltpu.SMEM)

    def params(mebibytes):
        return pltpu.CompilerParams(vmem_limit_bytes=mebibytes * 1024 * 1024)

    lists = candidate_blocks.T
    kinds = relation_offsets.reshape(1, count)
    codes = target_codes.reshape(1, count)

    vmem = pl.BlockSpec(memory_space=pltpu.VMEM)
    stride = depth // PARTS + 8
    spread = pl.pallas_call(
        query_kernel,
        out_shape=jax.ShapeDtypeStruct((owners * stride, count), bf16),
        in_specs=[smem] + [pl.BlockSpec(memory_space=pltpu.HBM)] * 2 + [vmem] * 2,
        scratch_shapes=[
            pltpu.VMEM((count, depth), f32),
            pltpu.VMEM(relations.shape, f32),
            pltpu.SemaphoreType.DMA,
            pltpu.SemaphoreType.DMA,
        ],
        compiler_params=params(61),
        name="query",
    )(head_offsets, table, relations, kinds, codes)
    held = lax.all_to_all(spread.reshape(owners, stride, count), "entity", 0, 0, tiled=True)

    share_rows = owners // 2 * 16
    slots, mine, matches = pl.pallas_call(
        plan_kernel,
        out_shape=(
            jax.ShapeDtypeStruct((PARTS, 128), i32),
            jax.ShapeDtypeStruct((16, 128), f32),
            jax.ShapeDtypeStruct((2, share_rows, 32), f32),
        ),
        in_specs=[smem] + [vmem] * 2,
        scratch_shapes=[pltpu.VMEM((owners, owners), f32)],
        compiler_params=params(8),
        name="plan",
    )(me, lists, list_lengths)

    held, rounded = lax.optimization_barrier((held, table.astype(bf16)))

    def pack(*refs):
        pack_kernel(*refs, block_rows)

    packed, targets = pl.pallas_call(
        pack,
        out_shape=(
            jax.ShapeDtypeStruct((depth, CAP * count), bf16),
            jax.ShapeDtypeStruct((16, count), i32),
        ),
        in_specs=[smem, smem] + [vmem] * 2,
        scratch_shapes=[pltpu.VMEM((16, count), f32)],
        compiler_params=params(8),
        name="pack",
    )(me, slots, held.reshape(owners * stride, count), mine)
    planes = [[z * PARTS + p for p in range(PARTS)] for z in range(owners // PARTS)]
    query_t = lax.all_to_all(
        packed.reshape(PARTS, depth // PARTS, CAP * count),
        "entity",
        0,
        0,
        tiled=True,
        axis_index_groups=planes,
    ).reshape(depth, CAP * count)
    assert groups == 4
    up = [(i, (i + 1) % groups) for i in range(groups)]
    down = [(i, (i - 1) % groups) for i in range(groups)]
    last_t, next_t = lax.ppermute(query_t, "dp", up), lax.ppermute(query_t, "dp", down)

    local = pl.pallas_call(
        stats_kernel,
        out_shape=jax.ShapeDtypeStruct((32, count), f32),
        in_specs=[vmem] * 3,
        scratch_shapes=[pltpu.VMEM((8, CAP * count), f32)] * 3,
        compiler_params=params(16),
        name="stats",
    )(query_t, rounded, targets)

    other = lax.ppermute(local, "entity", [(i, i ^ 1) for i in range(owners)])
    share = pl.pallas_call(
        share_kernel,
        out_shape=jax.ShapeDtypeStruct((share_rows, count), f32),
        in_specs=[vmem] * 3,
        compiler_params=params(8),
        name="share",
    )(matches, local, other)
    _, relay_last, relay_next = lax.optimization_barrier((share, last_t, next_t))
    far_low = lax.ppermute(relay_last[: depth // 2], "dp", up)
    far_high = lax.ppermute(relay_next[depth // 2 :], "dp", down)
    cores = [[i for i in range(owners) if i % 2 == core] for core in range(2)]
    shared = lax.all_to_all(
        share.reshape(owners // 2, 16, count), "entity", 0, 0, tiled=True, axis_index_groups=cores
    )

    info, loss = pl.pallas_call(
        merge_kernel,
        out_shape=(jax.ShapeDtypeStruct((groups, 32, count), f32), jax.ShapeDtypeStruct((1, count), f32)),
        compiler_params=params(8),
        name="merge",
    )(shared, targets)

    quarter = block_rows // groups
    half = quarter // 2
    mine_first = group.reshape(1)
    infos = lax.all_to_all(info, "dp", 0, 0, tiled=True)

    def cost(several):
        return pl.CostEstimate(
            flops=several * 4 * quarter * CAP * count * depth,
            transcendentals=several * quarter * CAP * count,
            bytes_accessed=8 * quarter * depth + several * 2 * CAP * count * depth,
        )

    own = pl.pallas_call(
        own_kernel,
        out_shape=jax.ShapeDtypeStruct((quarter, depth), f32),
        in_specs=[smem] + [vmem] * 3,
        scratch_shapes=[pltpu.VMEM((half, CAP * count), bf16)],
        compiler_params=params(16),
        cost_estimate=cost(1),
        name="own",
    )(mine_first, info, rounded, query_t)
    gradient = pl.pallas_call(
        rest_kernel,
        out_shape=jax.ShapeDtypeStruct((quarter, depth), f32),
        in_specs=[smem] + [vmem] * 2 + [pl.BlockSpec(memory_space=pltpu.HBM)] * 5,
        out_specs=pl.BlockSpec(memory_space=pltpu.HBM),
        scratch_shapes=[
            pltpu.VMEM((quarter, depth), f32),
            pltpu.VMEM((groups - 1, depth, CAP * count), bf16),
            pltpu.VMEM((half, CAP * count), bf16),
            pltpu.SemaphoreType.DMA((groups,)),
            pltpu.SemaphoreType.DMA,
            pltpu.SemaphoreType.DMA((2,)),
        ],
        input_output_aliases={3: 0},
        compiler_params=params(16),
        cost_estimate=cost(groups - 1),
        name="rest",
    )(mine_first, infos, rounded, own, next_t, last_t, far_low, far_high)
    return (loss.reshape(count), gradient[None])


def solution(mesh):
    return jax.shard_map(
        per_device,
        mesh=mesh,
        in_specs=(
            P("entity", None, None),
            P("entity", None, None),
            P("dp", None),
            P("dp", None),
            P(("dp", "entity")),
            P(("dp", "entity")),
            P(("dp", "entity")),
        ),
        out_specs=(P(("dp", "entity")), P("entity", "dp", None)),
        check_vma=False,
    )
```
